32 devices in a mesh: gx: 2 (over y), gy: 4 (over x, core), gz: 4 (over z).
Axes of the slice: x: 2, y: 2, z: 4, core: 2. Of those that a mesh axis runs over, the one named last changes fastest.
Arguments:
- features: float32 [2, 4, 4, 1920, 256], P('gx', 'gy', 'gz'), may hold values from -6 to 6
- slot_voxel: int32 [2, 4, 4, 1920], P('gx', 'gy', 'gz'), may hold values from 0 to 2047, as said below
- block_count: int32 [2, 4, 4], P('gx', 'gy', 'gz'), may hold values from 1 to 15, as said below
- hilbert_dest: int32 [2, 4, 4, 15], P('gx', 'gy', 'gz'), may hold values from -1 to 127, as said below
- transposed_dest: int32 [2, 4, 4, 30], P('gx', 'gy', 'gz'), may hold values from -1 to 127, as said below
- conv_weight: bfloat16 [2, 27, 256, 256], replicated, may hold values from -0.078125 to 0.078125
- qkv_weight: bfloat16 [2, 256, 768], replicated
- proj_weight: bfloat16 [2, 256, 256], replicated, may hold values from -0.375 to 0.375
- up_weight: bfloat16 [2, 256, 1024], replicated, may hold values from -0.375 to 0.375
- down_weight: bfloat16 [2, 1024, 256], replicated, may hold values from -0.1875 to 0.1875
Outputs:
- encoded: float32 [2, 4, 4, 1920, 256], P('gx', 'gy', 'gz')
The draws below stay inside these ranges and needn't reach their ends.
Inputs may be any that keep to these rules, and one draw needn't show every extreme that they name: `slot_voxel`: within one device the slots carry distinct voxel numbers. `block_count`: along gz, the counts of the devices of one (gx, gy) column sum to 8 times the size of gz; some device holds 15 blocks. `hilbert_dest`: -1 for block j at or past the device's block count, else o * 8 + p with 0 <= p < 8, o numbering the devices of the same gx index as gy index times the size of gz plus gz index. Every such owner and position receives exactly one block; no device sends more than 1 block to one owner, and some device sends 1. `transposed_dest`: -1 for half block h at or past twice the device's block count, else o 2 * 8 + p with 0 <= p < 16, o numbering the devices of the same gy index as gx index times the size of gz plus gz index. Every such owner and position receives exactly one half block; no device sends more than 4 half block to one owner, and some device sends 4.
All inputs are finite; a program needn't handle non-finite values.
Results may differ from the reference program's by a relative error of at most 0.025.
Values may be sent and summed in bfloat16 or wider, within the bound.
No kernel may reach another device: no remote copies, remote signals or barrier semaphores. Data moves between devices by JAX's collectives and lax.ppermute only.
A program may use at most 128 MiB of HBM per device.

```python
import math
import jax
import jax.numpy as jnp
from jax import lax

D = 256
HEADS = 16
FF = 1024
BLOCK = 128
VX = 16
VY = 16
VZ = 8
KMEAN = 8
KSLOTS = 15
SLOTS = 1920
PATCH = 1024
N_GX = 2
N_GY = 4
N_GZ = 4
DEVICES = 32


def column_counts(base_key):
    column_total = N_GX * N_GY
    key_order, key_size, key_pick = jax.random.split(base_key, 3)
    shuffles = jax.vmap(lambda sub_key: jax.random.permutation(sub_key, N_GZ))(jax.random.split(key_order, column_total))
    amplitude = jax.random.randint(key_size, (column_total, N_GZ // 2), 0, KMEAN)
    chosen = jax.random.randint(key_pick, (), 0, column_total)
    amplitude = amplitude.at[chosen, 0].set(KMEAN - 1)
    signed = jnp.concatenate([amplitude, -amplitude], axis=1)
    shifted = jnp.take_along_axis(signed, shuffles, axis=1)
    return (KMEAN + shifted).astype(jnp.int32).reshape(N_GX, N_GY, N_GZ)


def deal_group(group_key, member_counts, slot_total, per_owner):
    members = member_counts.shape[0]
    key_curve, key_label = jax.random.split(group_key)
    visiting = jax.random.permutation(key_curve, members)
    relabel = jax.random.permutation(key_label, members).astype(jnp.int32)
    ordered = member_counts[visiting]
    ordered_starts = (jnp.cumsum(ordered) - ordered).astype(jnp.int32)
    starts = jnp.zeros((members,), jnp.int32).at[visiting].set(ordered_starts)
    local_slot = jnp.arange(slot_total, dtype=jnp.int32)
    dealt = starts[:, None] + local_slot[None, :]
    owner_index = relabel[dealt % members]
    placed = owner_index * per_owner + dealt // members
    return jnp.where(local_slot[None, :] < member_counts[:, None], placed, -1).astype(jnp.int32)


def draw_block_count(key, part):
    return column_counts(jax.random.fold_in(key, 101))


def draw_hilbert_dest(key, part):
    counts = column_counts(jax.random.fold_in(key, 101))
    grouped = counts.reshape(N_GX, N_GY * N_GZ)
    group_keys = jax.random.split(jax.random.fold_in(key, 202), N_GX)
    dealt = jax.vmap(lambda group_key, member_counts: deal_group(group_key, member_counts, KSLOTS, KMEAN))(group_keys, grouped)
    return dealt.reshape(N_GX, N_GY, N_GZ, KSLOTS)


def draw_transposed_dest(key, part):
    counts = column_counts(jax.random.fold_in(key, 101))
    grouped = 2 * jnp.transpose(counts, (1, 0, 2)).reshape(N_GY, N_GX * N_GZ)
    group_keys = jax.random.split(jax.random.fold_in(key, 303), N_GY)
    dealt = jax.vmap(lambda group_key, member_counts: deal_group(group_key, member_counts, 2 * KSLOTS, 2 * KMEAN))(group_keys, grouped)
    return jnp.transpose(dealt.reshape(N_GY, N_GX, N_GZ, 2 * KSLOTS), (1, 0, 2, 3))


def draw_slot_voxel(key, part):
    device_keys = jax.random.split(jax.random.fold_in(key, 404), DEVICES)
    chosen = jax.vmap(lambda device_key: jax.random.permutation(device_key, VX * VY * VZ)[:SLOTS])(device_keys)
    return chosen.astype(jnp.int32).reshape(N_GX, N_GY, N_GZ, SLOTS)


def draw_qkv_weight(key, part):
    normal_draw = jax.random.normal(jax.random.fold_in(key, 505), (2, D, 3 * D), jnp.float32) / math.sqrt(D)
    column = jnp.arange(3 * D)
    scaled = normal_draw * jnp.where(column < 2 * D, 2.0, 1.0)
    return scaled.astype(jnp.bfloat16)


def steps_of(own_key, dims, cuts, least, high):
    level = 1.0
    for position, parts in cuts:
        steps = jax.random.uniform(jax.random.fold_in(jax.random.fold_in(own_key, 6), position), (parts,), jnp.float32, least / len(cuts), high / len(cuts))
        level = level * jnp.repeat(jnp.exp(steps), dims[position] // parts).reshape((-1,) + (1,) * (len(dims) - 1 - position))
    return level


def normal_values(stream_key, dims, deviation, bound, cuts=(), kind=jnp.bfloat16):
    values = jax.random.normal(stream_key, dims, jnp.float32) * deviation
    if len(cuts) > 0:
        values = steps_of(stream_key, dims, cuts, -0.22, 0.18) * values
    return jnp.clip(values, min=-bound, max=bound).astype(kind)


def setup_inputs(seed: int = 0) -> dict:
    key_list = jax.random.split(jax.random.key(seed), 11)
    features = normal_values(key_list[0], (N_GX, N_GY, N_GZ, SLOTS, D), 1.0, 6.0, ((0, 2), (1, 4), (2, 4)), jnp.float32)
    slot_voxel = draw_slot_voxel(jax.random.fold_in(key_list[10], 71), 0)
    block_count = draw_block_count(jax.random.fold_in(key_list[10], 71), 0)
    hilbert_dest = draw_hilbert_dest(jax.random.fold_in(key_list[10], 71), 0)
    transposed_dest = draw_transposed_dest(jax.random.fold_in(key_list[10], 71), 0)
    conv_weight = normal_values(key_list[5], (2, 27, D, D), (27 * D) ** -0.5, 0.078125)
    qkv_weight = draw_qkv_weight(jax.random.fold_in(key_list[10], 71), 0)
    proj_weight = normal_values(key_list[7], (2, D, D), D ** -0.5, 0.375)
    up_weight = normal_values(key_list[8], (2, D, FF), D ** -0.5, 0.375)
    down_weight = normal_values(key_list[9], (2, FF, D), FF ** -0.5, 0.1875)
    return dict(features=features, slot_voxel=slot_voxel, block_count=block_count, hilbert_dest=hilbert_dest, transposed_dest=transposed_dest, conv_weight=conv_weight, qkv_weight=qkv_weight, proj_weight=proj_weight, up_weight=up_weight, down_weight=down_weight)


EPS = 1e-05

def layer_norm(values):
    centred = values - lax.optimization_barrier(jnp.mean(values, axis=-1, keepdims=True))
    variance = lax.optimization_barrier(jnp.mean(centred * centred, axis=-1, keepdims=True))
    return centred * lax.rsqrt(variance + EPS)

def attend_patch(patch_rows, qkv_matrix, out_matrix):
    patch_len, channels = patch_rows.shape
    head_width = channels // HEADS
    normed = layer_norm(patch_rows).astype(jnp.bfloat16)
    packed = jnp.dot(normed, qkv_matrix, preferred_element_type=jnp.float32).astype(jnp.bfloat16)
    packed = packed.reshape(patch_len, 3, HEADS, head_width).astype(jnp.float32)
    query_rows = jnp.transpose(packed[:, 0], (1, 0, 2))
    key_entries = jnp.transpose(packed[:, 1], (1, 0, 2))
    value_entries = jnp.transpose(packed[:, 2], (1, 0, 2))
    logit_scores = jnp.einsum('eyj,esj->eys', query_rows, key_entries) * (1.0 / math.sqrt(head_width))
    row_max = lax.optimization_barrier(jnp.max(logit_scores, axis=-1, keepdims=True))
    exp_scores = jnp.exp(logit_scores - row_max)
    attention_weights = (exp_scores / lax.optimization_barrier(jnp.sum(exp_scores, axis=-1, keepdims=True))).astype(jnp.bfloat16)
    head_result = jnp.einsum('ver,vrs->ves', attention_weights.astype(jnp.float32), value_entries).astype(jnp.bfloat16)
    merged = jnp.transpose(head_result, (1, 0, 2)).reshape(patch_len, channels)
    return patch_rows + jnp.dot(merged, out_matrix, preferred_element_type=jnp.float32)

def feed_forward(point_rows, up_matrix, down_matrix):
    normed = layer_norm(point_rows).astype(jnp.bfloat16)
    hidden = jax.nn.gelu(jnp.dot(normed, up_matrix, preferred_element_type=jnp.float32), approximate=False).astype(jnp.bfloat16)
    return point_rows + jnp.dot(hidden, down_matrix, preferred_element_type=jnp.float32)

def reference(features, slot_voxel, block_count, hilbert_dest, transposed_dest, conv_weight, qkv_weight, proj_weight, up_weight, down_weight):
    plane_size = N_GY * N_GZ
    total_blocks = DEVICES * KMEAN
    channels = features.shape[-1]
    counts = block_count.reshape(DEVICES).astype(jnp.int32)
    block_ends = jnp.cumsum(counts).astype(jnp.int32)
    starts = block_ends - counts
    block_index = jnp.arange(total_blocks, dtype=jnp.int32)
    device = jnp.searchsorted(block_ends, block_index, side='right').astype(jnp.int32)
    local_block = block_index - starts[device]
    flat_block = device * KSLOTS + local_block
    stream = features.reshape(DEVICES * KSLOTS, BLOCK, channels)[flat_block].reshape(-1, channels)
    voxels = slot_voxel.reshape(DEVICES * KSLOTS, BLOCK)[flat_block].reshape(-1)
    point_device = jnp.repeat(device, BLOCK)
    coord_x = point_device // plane_size * VX + voxels // (VY * VZ) + 1
    coord_y = point_device // N_GZ % N_GY * VY + voxels // VZ % VY + 1
    coord_z = point_device % N_GZ * VZ + voxels % VZ + 1
    span_y = N_GY * VY + 2
    span_z = N_GZ * VZ + 2
    cell_count = (N_GX * VX + 2) * span_y * span_z
    points = total_blocks * BLOCK
    home_cell = ((coord_x * span_y + coord_y) * span_z + coord_z).astype(jnp.int32)
    lookup = jnp.full((cell_count,), points, jnp.int32).at[home_cell].set(jnp.arange(points, dtype=jnp.int32))

    def convolve(current, attention_weights):
        zero_padded = jnp.concatenate([current.astype(jnp.bfloat16), jnp.zeros((1, channels), jnp.bfloat16)], axis=0)

        def offset_step(running, offset_item):
            offset, weight = offset_item
            displace = (offset // 9 - 1) * span_y * span_z + (offset // 3 % 3 - 1) * span_z + (offset % 3 - 1)
            neighbours = zero_padded[lookup[home_cell + displace]]
            return (running + jnp.dot(neighbours, weight, preferred_element_type=jnp.float32), None)
        running, unused = lax.scan(offset_step, jnp.zeros((points, channels), jnp.float32), (jnp.arange(27, dtype=jnp.int32), attention_weights))
        return running
    dest_first = hilbert_dest.reshape(DEVICES * KSLOTS)[flat_block]
    owner_first = device // plane_size * plane_size + dest_first // KMEAN
    target_first = owner_first * KMEAN + dest_first % KMEAN
    order_first = jnp.zeros((total_blocks,), jnp.int32).at[target_first].set(block_index)
    halves = jnp.arange(2 * total_blocks, dtype=jnp.int32)
    half_block = halves // 2
    dest_second = transposed_dest.reshape(DEVICES * 2 * KSLOTS)[2 * flat_block[half_block] + halves % 2]
    group_owner = dest_second // (2 * KMEAN)
    owner_second = group_owner // N_GZ * plane_size + device[half_block] // N_GZ % N_GY * N_GZ + group_owner % N_GZ
    target_second = owner_second * (2 * KMEAN) + dest_second % (2 * KMEAN)
    order_second = jnp.zeros((2 * total_blocks,), jnp.int32).at[target_second].set(halves)
    for layer_index in range(2):
        stream = stream + layer_norm(convolve(stream, conv_weight[layer_index]))
        if layer_index == 0:
            order_now = order_first
            unit_rows = BLOCK
        else:
            order_now = order_second
            unit_rows = BLOCK // 2
        pieces = stream.reshape(-1, unit_rows, channels)[order_now].reshape(-1, PATCH, channels)
        qkv_now = qkv_weight[layer_index]
        proj_now = proj_weight[layer_index]
        attended = lax.map(lambda patch_rows: attend_patch(patch_rows, qkv_now, proj_now), pieces)
        stream = jnp.zeros((points // unit_rows, unit_rows, channels), jnp.float32).at[order_now].set(attended.reshape(-1, unit_rows, channels)).reshape(points, channels)
        stream = feed_forward(stream, up_weight[layer_index], down_weight[layer_index])
    result = jnp.zeros((DEVICES * KSLOTS, BLOCK, channels), jnp.float32).at[flat_block].set(stream.reshape(-1, BLOCK, channels))
    return result.reshape(N_GX, N_GY, N_GZ, KSLOTS * BLOCK, channels)
```

```python
import functools
import math

import jax
import jax.numpy as jnp
from jax import lax
from jax.experimental import pallas as pl
from jax.experimental.pallas import tpu as pltpu
from jax.sharding import PartitionSpec as P

HEADS = 16
PATCH = 1024
VX = 16
VY = 16
VZ = 8
PX = VX + 2
PZ = 16
CELLS = VX * VY * VZ
PLANE = PX * PZ
EPS = 1e-05
CLIP = 3e38
HELD = 12
F32 = jnp.float32
BF16 = jnp.bfloat16
SMEM = pltpu.MemorySpace.SMEM


def call(kernel, outs, ins, scratch=(), name=None, limit=24, flops=0):
    spaces = {"s": SMEM, "v": pltpu.MemorySpace.VMEM, "h": pltpu.MemorySpace.HBM}

    def spec(where):
        return pl.BlockSpec(memory_space=spaces[where]) if isinstance(where, str) else where

    windowed = any(not isinstance(where, str) for _, where in ins)
    result = pl.pallas_call(
        kernel,
        out_shape=tuple(shape for shape, _ in outs),
        grid=(1,) if windowed else (),
        in_specs=[spec(where) for _, where in ins],
        out_specs=tuple(spec(where) for _, where in outs),
        scratch_shapes=list(scratch),
        name=name,
        cost_estimate=pl.CostEstimate(flops=flops, transcendentals=0, bytes_accessed=1 << 20) if flops else None,
        compiler_params=pltpu.CompilerParams(vmem_limit_bytes=limit * 1024 * 1024),
    )(*(array for array, _ in ins))
    return result if len(outs) > 1 else result[0]


def row_groups(rows):
    return next(g for g in (5, 4, 3, 2, 1) if rows % (g * 128) == 0)


def group_copies(src_ref, dst_ref, sems):
    groups = sems.shape[0]
    size = min(src_ref.shape[0], dst_ref.shape[0]) // groups
    parts = [slice(g * size, (g + 1) * size) for g in range(groups)]
    return parts, [pltpu.make_async_copy(src_ref.at[p], dst_ref.at[p], sems.at[g]) for g, p in enumerate(parts)]


def weight_copies(layer, w_ref, dst_ref, sems):
    return [pltpu.make_async_copy(w_ref.at[layer, pl.ds(9 * da, 9)], dst_ref.at[pl.ds(9 * da, 9)], sems.at[da]) for da in range(3)]


def tap(w_ref, da, db, dc):
    return w_ref[9 * da + 3 * db + dc]


def sds(shape, dtype):
    return jax.ShapeDtypeStruct(shape, dtype)


def layer_norm(values):
    centred = values - jnp.mean(values, axis=-1, keepdims=True)
    variance = jnp.mean(centred * centred, axis=-1, keepdims=True)
    return centred * lax.rsqrt(variance + EPS)


def iota(shape, dim):
    return lax.broadcasted_iota(jnp.int32, shape, dim)


def cell_of(voxel):
    x = voxel // (VY * VZ)
    y = (voxel // VZ) % VY
    z = voxel % VZ
    return (x * VZ + z) * VY + y


def voxel_row(vox_ref):
    return jnp.concatenate([vox_ref[j] for j in range(vox_ref.shape[0])], axis=1)


def onehot(mask):
    return jnp.where(mask, 1.0, 0.0).astype(BF16)


def assign_slots(dest_ref, count_ref, slot_ref, used_ref, owners, capacity, per_owner, units_per_block):
    units = dest_ref.shape[0]

    def clear(o, c):
        used_ref[o] = 0
        return c

    lax.fori_loop(0, owners, clear, 0)

    def step(j, c):
        owner = jnp.maximum(dest_ref[j], 0) // per_owner
        rank = used_ref[owner]
        slot_ref[j] = jnp.minimum(owner * capacity + rank, owners * capacity - 1)
        used_ref[owner] = rank + 1
        return c

    lax.fori_loop(0, jnp.minimum(count_ref[0] * units_per_block, units), step, 0)


def place(rows_ref, ids, flags_ref, own_ref, xmsg_ref, ymsg_ref):
    slots = rows_ref.shape[0]
    tile = 256

    def one(t, c):
        r = iota((tile, slots), 0) + t * tile
        hot = onehot(r == ids)
        own_ref[pl.ds(pl.multiple_of(t * tile, tile), tile), :] = jnp.dot(
            hot, rows_ref[...], preferred_element_type=F32
        ).astype(BF16)
        return c

    lax.fori_loop(0, CELLS // tile, one, 0)
    face_rows = VZ * VY
    low, high = own_ref[0:face_rows], own_ref[CELLS - face_rows : CELLS]
    if xmsg_ref.shape[0] == 1:
        xmsg_ref[0] = jnp.where(flags_ref[1] > 0, high, low)
    else:
        xmsg_ref[0] = low
        xmsg_ref[1] = high
    for face in range(2):
        r = iota((PLANE, 1), 0)
        x = r // PZ - 1
        z = r % PZ - 1
        inside = (x >= 0) & (x < VX) & (z >= 0) & (z < VZ)
        cell = jnp.where(inside, (x * VZ + z) * VY + (VY - 1) * face, -2)
        hot = onehot(cell == ids)
        ymsg_ref[face] = jnp.dot(hot, rows_ref[...], preferred_element_type=F32).astype(BF16)


def place_first_kernel(
    layer, block, flags_ref, count_ref, vox_ref, feat_ref, w_in_ref, own_ref, xmsg_ref, ymsg_ref, w_ref, rows_ref, wsems
):
    slots = feat_ref.shape[0]
    weights = weight_copies(layer, w_in_ref, w_ref, wsems)
    for copy in weights:
        copy.start()
    rows_ref[...] = feat_ref[...].astype(BF16)
    live = iota((1, slots), 1) < count_ref[0] * block
    ids = jnp.where(live, cell_of(voxel_row(vox_ref)), -1)
    place(rows_ref, ids, flags_ref, own_ref, xmsg_ref, ymsg_ref)
    for copy in weights:
        copy.wait()


def restore_unit(u, unit, live_units, slot_ref, first_ref, backs):
    alive = u < live_units
    slot = jnp.where(alive, slot_ref[u], 0)
    part = unit // len(backs)
    for k, back_ref in enumerate(backs):
        rows = pl.ds(pl.multiple_of(u * unit + k * part, part), part)
        total = first_ref[rows, :] + back_ref[slot].astype(F32)
        yield rows, jnp.where(alive, total, 0.0)


def place_next_kernel(
    layer,
    route,
    flags_ref,
    count_ref,
    dest_ref,
    vox_ref,
    first_ref,
    back_a_ref,
    back_b_ref,
    w_in_ref,
    own_ref,
    xmsg_ref,
    ymsg_ref,
    w_ref,
    stream_ref,
    rows_ref,
    first_vmem,
    slot_ref,
    used_ref,
    sems,
    wsems,
):
    owners, capacity, per_owner, units_per_block, unit = route
    slots = first_vmem.shape[0]
    parts, copies = group_copies(first_ref, first_vmem, sems)
    weights = weight_copies(layer, w_in_ref, w_ref, wsems)
    for copy in copies + weights:
        copy.start()
    assign_slots(dest_ref, count_ref, slot_ref, used_ref, owners, capacity, per_owner, units_per_block)
    live_units = count_ref[0] * units_per_block
    per = slots // unit // len(parts)

    def one(u, c):
        for rows, value in restore_unit(u, unit, live_units, slot_ref, first_vmem, (back_a_ref, back_b_ref)):
            stream_ref[rows, :] = value
            rows_ref[rows, :] = value.astype(BF16)
        return c

    for g, copy in enumerate(copies):
        copy.wait()
        lax.fori_loop(g * per, (g + 1) * per, one, 0)
    live = iota((1, slots), 1) < live_units * unit
    ids = jnp.where(live, cell_of(voxel_row(vox_ref)), -1)
    place(rows_ref, ids, flags_ref, own_ref, xmsg_ref, ymsg_ref)
    for copy in weights:
        copy.wait()


def restore_kernel(
    route, count_ref, dest_ref, first_ref, back_a_ref, back_b_ref, out_ref, first_vmem, out_vmem, slot_ref, used_ref, sems, osems
):
    owners, capacity, per_owner, units_per_block, unit = route
    parts, copies = group_copies(first_ref, first_vmem, sems)
    _, sends = group_copies(out_vmem, out_ref, osems)
    for copy in copies:
        copy.start()
    assign_slots(dest_ref, count_ref, slot_ref, used_ref, owners, capacity, per_owner, units_per_block)
    live_units = count_ref[0] * units_per_block
    per = first_vmem.shape[0] // unit // len(parts)

    def one(u, c):
        for rows, value in restore_unit(u, unit, live_units, slot_ref, first_vmem, (back_a_ref, back_b_ref)):
            out_vmem[rows, :] = value
        return c

    for g, copy in enumerate(copies):
        copy.wait()
        lax.fori_loop(g * per, (g + 1) * per, one, 0)
        sends[g].start()
    for send in sends:
        send.wait()


def masked(flag, values):
    return jnp.where(flag > 0, values, jnp.zeros_like(values))


def zface_kernel(after_ref, flags_ref, bottom_ref, top_ref, lo_ref, hi_ref, out_lo_ref, out_hi_ref):
    for out_ref, z, face_ref in ((out_lo_ref, 0, bottom_ref), (out_hi_ref, VZ - 1, top_ref)):
        out_ref[0] = masked(flags_ref[0], lo_ref[z])
        out_ref[PX - 1] = masked(flags_ref[1], hi_ref[z])
        out_ref[1 : 1 + VX] = face_ref[...]


def yface_kernel(after_ref, flags_ref, ymsg_ref, xlo_ref, xhi_ref, zlo_ref, zhi_ref, out_lo_ref, out_hi_ref, src_ref):
    nx = VZ * VY
    nz = PX * VY
    src_ref[...] = jnp.zeros_like(src_ref)
    src_ref[0:nx] = masked(flags_ref[0], xlo_ref[...].reshape(nx, -1))
    src_ref[nx : 2 * nx] = masked(flags_ref[1], xhi_ref[...].reshape(nx, -1))
    src_ref[2 * nx : 2 * nx + nz] = zlo_ref[...].reshape(nz, -1)
    src_ref[2 * nx + nz : 2 * nx + 2 * nz] = zhi_ref[...].reshape(nz, -1)
    r = iota((PLANE, 1), 0)
    x = r // PZ
    z = r % PZ
    inner = (z >= 1) & (z <= VZ)
    for out_ref, face in ((out_lo_ref, 0), (out_hi_ref, 1)):
        y = (VY - 1) * face
        want = jnp.where(inner & (x == 0), (z - 1) * VY + y, -1)
        want = jnp.where(inner & (x == PX - 1), nx + (z - 1) * VY + y, want)
        want = jnp.where(z == 0, 2 * nx + x * VY + y, want)
        want = jnp.where(z == VZ + 1, 2 * nx + nz + x * VY + y, want)
        hot = onehot(iota((PLANE, src_ref.shape[0]), 1) == want)
        extra = jnp.dot(hot, src_ref[...], preferred_element_type=F32)
        out_ref[...] = (ymsg_ref[face].astype(F32) + extra).astype(BF16)


def conv_tiles(w_ref, out_ref, pad_ref, start, stride, count, planes):
    channels = pad_ref.shape[-1]
    rows = planes * VZ * VY

    def one(t, c):
        x0 = start + t * stride
        parts = []
        for da in range(3):
            for dc in range(3):
                window = pad_ref[pl.ds(x0 + da, planes), dc : dc + VZ]
                parts.append(window.reshape(rows, channels))
        lhs = jnp.concatenate(parts, axis=1)
        accs = []
        for db in range(3):
            rhs = jnp.concatenate([tap(w_ref, da, db, dc) for da in range(3) for dc in range(3)], axis=0)
            accs.append(jnp.dot(lhs, rhs, preferred_element_type=F32).reshape(planes * VZ, VY, channels))
        out_ref[pl.ds(pl.multiple_of(t * rows, rows), rows), :] = shift_sum(accs).reshape(rows, channels).astype(BF16)
        return c

    lax.fori_loop(0, count, one, 0)


def shift_sum(accs):
    y = iota(accs[0].shape, 1)
    low = jnp.where(y == 0, 0.0, pltpu.roll(accs[0], 1, 1))
    high = jnp.where(y == VY - 1, 0.0, pltpu.roll(accs[2], VY - 1, 1))
    return low + accs[1] + high


def clear_z(pad_ref, x):
    edge = jnp.zeros(pad_ref.shape[2:], BF16)
    pad_ref[x, 0] = edge
    pad_ref[x, VZ + 1] = edge


def conv_middle_kernel(planes, own_ref, w_ref, out_ref, pad_ref):
    for x in range(planes - 1, VX - planes + 1):
        clear_z(pad_ref, x + 1)
        pad_ref[x + 1, 1 : 1 + VZ] = own_ref[x]
    conv_tiles(w_ref, out_ref, pad_ref, planes, planes, VX // planes - 2, planes)


def conv_ends_kernel(planes, flags_ref, own_ref, xlo_ref, xhi_ref, w_ref, out_ref, pad_ref):
    for x in list(range(planes + 1)) + list(range(VX - planes - 1, VX)):
        clear_z(pad_ref, x + 1)
        pad_ref[x + 1, 1 : 1 + VZ] = own_ref[x]
    for x, halo_ref, k in ((0, xlo_ref, 0), (PX - 1, xhi_ref, 1)):
        clear_z(pad_ref, x)
        pad_ref[x, 1 : 1 + VZ] = masked(flags_ref[k], halo_ref[...])
    conv_tiles(w_ref, out_ref, pad_ref, 0, VX - planes, 2, planes)


def conv_z_kernel(zlo_ref, zhi_ref, w_ref, out_ref):
    channels = zlo_ref.shape[-1]
    for face, halo_ref in ((0, zlo_ref), (1, zhi_ref)):
        lhs = jnp.concatenate([halo_ref[da : da + VX].reshape(VX * VY, channels) for da in range(3)], axis=1)
        accs = []
        for db in range(3):
            rhs = jnp.concatenate([tap(w_ref, da, db, 2 * face) for da in range(3)], axis=0)
            accs.append(jnp.dot(lhs, rhs, preferred_element_type=F32).reshape(VX, VY, channels))
        out_ref[face] = shift_sum(accs)


def conv_finish_kernel(
    planes,
    route,
    count_ref,
    dest_ref,
    vox_ref,
    middle_ref,
    ends_ref,
    zc_ref,
    lo_ref,
    hi_ref,
    w_ref,
    stream_ref,
    first_ref,
    send_ref,
    table_ref,
    first_vmem,
    slot_ref,
    used_ref,
    fsems,
):
    owners, capacity, per_owner, units_per_block, unit = route
    channels = middle_ref.shape[-1]
    assign_slots(dest_ref, count_ref, slot_ref, used_ref, owners, capacity, per_owner, units_per_block)
    for s in range(owners * capacity):
        send_ref[s, 0:16] = jnp.full((16, channels), jnp.inf, BF16)
    per_x = VZ * VY
    edge = planes * per_x
    table_ref[0:edge] = ends_ref[0:edge]
    table_ref[edge : CELLS - edge] = middle_ref[...]
    table_ref[CELLS - edge : CELLS] = ends_ref[edge:]
    for face, z in ((0, 0), (1, VZ - 1)):
        for x in range(VX):
            rows = slice(x * per_x + z * VY, x * per_x + (z + 1) * VY)
            table_ref[rows] = (table_ref[rows].astype(F32) + zc_ref[face, x]).astype(BF16)
    plane_rows = VX * PZ
    for face, plane_ref in ((0, lo_ref), (1, hi_ref)):
        plane = plane_ref[...].reshape(PX, PZ, channels)
        wide = plane.astype(F32)
        shifted = [plane] + [pltpu.roll(wide, PZ - dc, 1).astype(BF16) for dc in (1, 2)]
        parts = [shifted[dc][da : da + VX].reshape(plane_rows, channels) for da in range(3) for dc in range(3)]
        rhs = jnp.concatenate([tap(w_ref, da, 2 * face, dc) for da in range(3) for dc in range(3)], axis=0)
        out = jnp.dot(jnp.concatenate(parts, axis=1), rhs, preferred_element_type=F32)
        table_ref[CELLS + face * plane_rows : CELLS + (face + 1) * plane_rows] = out.astype(BF16)
    blocks, _, block = vox_ref.shape
    group = next(g for g in (3, 2, 1) if blocks % g == 0)
    live = count_ref[0]

    def hot_rows(j):
        v = vox_ref[j]
        vt = jnp.transpose(jnp.broadcast_to(v.astype(F32), (block, block))).astype(jnp.int32)
        x = vt // (VY * VZ)
        y = (vt // VZ) % VY
        z = vt % VZ
        main = (x * VZ + z) * VY + y
        lo = jnp.where(y == 0, CELLS + x * PZ + z, -1)
        hi = jnp.where(y == VY - 1, CELLS + plane_rows + x * PZ + z, -1)
        lane = iota((block, block), 1)
        pieces = []
        for k in range((CELLS + 2 * plane_rows) // block):
            ids = main if k * block < CELLS else (lo if k * block < CELLS + plane_rows else hi)
            pieces.append(onehot(ids == lane + k * block))
        return jnp.concatenate(pieces, axis=1)

    def one(g, c):
        hot = jnp.concatenate([hot_rows(g * group + i) for i in range(group)], axis=0)
        gathered = jnp.dot(hot, table_ref[...], preferred_element_type=F32)
        rows = pl.ds(pl.multiple_of(g * group * block, group * block), group * block)
        first = stream_ref[rows, :] + layer_norm(gathered)
        first_vmem[rows, :] = first
        pltpu.make_async_copy(first_vmem.at[rows], first_ref.at[rows], fsems.at[g]).start()
        packed = jnp.clip(first, -CLIP, CLIP).astype(BF16)
        for i in range(group):
            j = g * group + i

            @pl.when(j < live)
            def _():
                for k in range(units_per_block):
                    low = i * block + k * unit
                    send_ref[slot_ref[j * units_per_block + k]] = packed[low : low + unit]

        return c

    lax.fori_loop(0, blocks // group, one, 0)
    for g in range(blocks // group):
        rows = slice(g * group * block, (g + 1) * group * block)
        pltpu.make_async_copy(first_vmem.at[rows], first_ref.at[rows], fsems.at[g]).wait()


def attend_and_feed(x_ref, q_ref, kt_ref, va_ref, vb_ref, proj_ref, up_ref, down_ref, heads_ref, s0_ref, s1_ref, delta_ref):
    tile, channels = q_ref.shape
    half = channels // 2
    width = channels // HEADS
    scale = math.log2(math.e) / math.sqrt(width)
    group = iota((tile, half), 1) // width

    def score(h, side):
        cols = slice(side * half, (side + 1) * half)
        q = jnp.where(group == h, q_ref[:, cols].astype(F32), 0.0).astype(BF16)
        return jnp.dot(q, kt_ref[cols, :], preferred_element_type=F32)

    def combine(h, side, scores):
        cols = slice(side * half, (side + 1) * half)
        v_ref = (va_ref, vb_ref)[side]
        top = jnp.max(scores, axis=-1, keepdims=True)
        probs = jnp.exp2(((scores - top) * scale).astype(BF16))
        res = jnp.dot(probs, v_ref[...], preferred_element_type=F32)
        heads_ref[:, cols] = jnp.where(group == h, res[:, :half] / res[:, half:], heads_ref[:, cols])

    s0_ref[...] = score(0, 0)

    def head(h, c):
        s1_ref[...] = score(h, 1)
        combine(h, 0, s0_ref[...])
        s0_ref[...] = score(h + 1, 0)
        combine(h, 1, s1_ref[...])
        return c

    lax.fori_loop(0, half // width, head, 0)
    x = x_ref[0:tile, :].astype(F32)
    update = jnp.dot(heads_ref[...].astype(BF16), proj_ref[...], preferred_element_type=F32)
    normed = layer_norm(x + update).astype(BF16)
    hidden = jnp.dot(normed, up_ref[...], preferred_element_type=F32)
    hidden = (0.5 * hidden * (1.0 + lax.erf(hidden * (1.0 / math.sqrt(2.0))))).astype(BF16)
    delta_ref[...] = (update + jnp.dot(hidden, down_ref[...], preferred_element_type=F32)).astype(BF16)


def with_ones(v_ref, va_ref, vb_ref):
    rows, channels = v_ref.shape
    half = channels // 2
    ones = jnp.ones((rows, half), BF16)
    for side, ref in ((0, va_ref), (1, vb_ref)):
        ref[:, :half] = v_ref[:, side * half : (side + 1) * half]
        ref[:, half:] = ones


def answer_copies(pos_ref, delta_ref, out_ref, sems):
    slots, part, _ = out_ref.shape
    copies = []
    for s in range(slots):
        rows = pl.ds(pl.multiple_of(pos_ref[s] * part, part), part)
        copies.append(pltpu.make_async_copy(delta_ref.at[rows], out_ref.at[s], sems.at[s]))
        copies[-1].start()
    return copies


def owner_a_kernel(
    layer,
    recv_in_ref,
    qkv_in_ref,
    proj_in_ref,
    up_in_ref,
    down_in_ref,
    out_ref,
    xb_out_ref,
    qb_out_ref,
    kt_out_ref,
    v_out_ref,
    pos_ref,
    xa_ref,
    xb_ref,
    qa_ref,
    qb_ref,
    kt_ref,
    v_ref,
    va_ref,
    vb_ref,
    heads_ref,
    delta_ref,
    s0_ref,
    s1_ref,
    sems,
    osems,
    recv_ref,
    proj_ref,
    up_ref,
    down_ref,
    wsems,
    qkv_ref,
):
    pairs = ((qkv_in_ref, qkv_ref), (proj_in_ref, proj_ref), (up_in_ref, up_ref), (down_in_ref, down_ref))
    weights = [pltpu.make_async_copy(src.at[layer], dst, wsems.at[k]) for k, (src, dst) in enumerate(pairs)]
    arrival = pltpu.make_async_copy(recv_in_ref, recv_ref, osems.at[0])
    arrival.start()
    for copy in weights:
        copy.start()
    slots, unit, channels = recv_ref.shape
    part = unit // 2
    units = PATCH // unit
    tile = PATCH // 2
    pos = jnp.int32(0)
    arrival.wait()
    for s in range(slots):
        mark = jnp.max(recv_ref[s, 0:16, 0:128].astype(F32))
        pos_ref[s] = jnp.minimum(pos, units - 1)
        rows = pl.ds(pl.multiple_of(pos * part, part), part)
        xa_ref[rows, :] = recv_ref[s, :part]
        xb_ref[rows, :] = recv_ref[s, part:]
        pos = jnp.minimum(pos + jnp.where(mark > CLIP * 1.1, 0, 1), units)
    step = 256
    weights[0].wait()
    for c, (src_ref, dst_ref) in enumerate(((xa_ref, qa_ref), (xb_ref, qb_ref))):
        for t in range(tile // step):
            rows = slice(t * step, (t + 1) * step)
            both = slice(c * tile + t * step, c * tile + (t + 1) * step)
            normed = layer_norm(src_ref[rows, :].astype(F32)).astype(BF16)
            packed = jnp.dot(normed, qkv_ref[...], preferred_element_type=F32)
            dst_ref[rows, :] = packed[:, :channels].astype(BF16)
            kt_ref[:, both] = jnp.transpose(packed[:, channels : 2 * channels]).astype(BF16)
            v_ref[both, :] = packed[:, 2 * channels :].astype(BF16)
    pairs = ((xb_ref.at[0:tile], xb_out_ref), (qb_ref, qb_out_ref), (kt_ref, kt_out_ref), (v_ref, v_out_ref))
    handed = [pltpu.make_async_copy(src, dst, sems.at[k]) for k, (src, dst) in enumerate(pairs)]
    for copy in handed:
        copy.start()
    with_ones(v_ref, va_ref, vb_ref)
    for copy in weights[1:]:
        copy.wait()
    attend_and_feed(
        xa_ref, qa_ref, kt_ref, va_ref, vb_ref, proj_ref, up_ref, down_ref, heads_ref, s0_ref, s1_ref, delta_ref
    )
    for copy in handed + answer_copies(pos_ref, delta_ref, out_ref, osems):
        copy.wait()


def owner_b_kernel(
    layer,
    pos_ref,
    x_in_ref,
    q_in_ref,
    kt_in_ref,
    v_in_ref,
    proj_in_ref,
    up_in_ref,
    down_in_ref,
    out_ref,
    x_ref,
    q_ref,
    kt_ref,
    v_ref,
    va_ref,
    vb_ref,
    heads_ref,
    delta_ref,
    s0_ref,
    s1_ref,
    sems,
    osems,
    proj_ref,
    up_ref,
    down_ref,
    wsems,
):
    pairs = ((proj_in_ref, proj_ref), (up_in_ref, up_ref), (down_in_ref, down_ref))
    weights = [pltpu.make_async_copy(src.at[layer], dst, wsems.at[k]) for k, (src, dst) in enumerate(pairs)]
    pairs = ((q_in_ref, q_ref), (kt_in_ref, kt_ref), (v_in_ref, v_ref), (x_in_ref, x_ref))
    copies = [pltpu.make_async_copy(src, dst, sems.at[k]) for k, (src, dst) in enumerate(pairs)]
    for copy in copies + weights:
        copy.start()
    for copy in copies + weights:
        copy.wait()
    with_ones(v_ref, va_ref, vb_ref)
    attend_and_feed(x_ref, q_ref, kt_ref, va_ref, vb_ref, proj_ref, up_ref, down_ref, heads_ref, s0_ref, s1_ref, delta_ref)
    for copy in answer_copies(pos_ref, delta_ref, out_ref, osems):
        copy.wait()


def owner_work(received, layer, qkv_weight, proj_weight, up_weight, down_weight):
    slots, unit, channels = received.shape
    tile = PATCH // 2
    part = unit // 2
    arrays = (qkv_weight, proj_weight, up_weight, down_weight)
    weights = [(w, "h") for w in arrays]
    held_weights = [pltpu.VMEM(w.shape[1:], BF16) for w in arrays]
    half = pltpu.VMEM((tile, channels), BF16)
    whole = pltpu.VMEM((PATCH, channels), BF16)
    across = pltpu.VMEM((channels, PATCH), BF16)
    held = pltpu.VMEM((tile + part, channels), BF16)
    scores = pltpu.VMEM((tile, PATCH), F32)
    tail = [across, whole, whole, whole, pltpu.VMEM((tile, channels), F32), half, scores, scores]
    tail += [pltpu.SemaphoreType.DMA((4,)), pltpu.SemaphoreType.DMA((slots,))]
    answer = (sds((slots, part, channels), BF16), "h")
    rows = (sds((tile, channels), BF16), "h")
    out_a, xb, qb, kt, v, pos = call(
        functools.partial(owner_a_kernel, layer),
        [answer, rows, rows, (sds((channels, PATCH), BF16), "h"), (sds((PATCH, channels), BF16), "h")]
        + [(sds((slots,), jnp.int32), "s")],
        [(received, "h")] + weights,
        [held, held, half, half]
        + tail
        + [pltpu.VMEM(received.shape, BF16)]
        + held_weights[1:]
        + [pltpu.SemaphoreType.DMA((4,)), held_weights[0]],
        "owner_a",
        61,
        1 << 33,
    )
    out_b = call(
        functools.partial(owner_b_kernel, layer),
        [answer],
        [(pos, "s"), (xb, "h"), (qb, "h"), (kt, "h"), (v, "h")] + weights[1:],
        [half, half] + tail + held_weights[1:] + [pltpu.SemaphoreType.DMA((3,))],
        "owner_b",
        61,
        1 << 33,
    )
    return out_a, out_b


def up_down(axis, low_face, high_face):
    count = lax.axis_size(axis)
    ends = count - 1
    from_low = lax.ppermute(high_face, axis, [(i, (i + 1) % count) for i in range(ends)])
    from_high = lax.ppermute(low_face, axis, [((i + 1) % count, i) for i in range(ends)])
    return from_low, from_high


def exchange_x(faces):
    if faces.shape[0] == 1:
        got = lax.ppermute(faces, "gx", [(0, 1), (1, 0)]).reshape(faces.shape[1:])
        return got, got
    return up_down("gx", faces[0], faces[1])


def body(
    features,
    slot_voxel,
    block_count,
    hilbert_dest,
    transposed_dest,
    conv_weight,
    qkv_weight,
    proj_weight,
    up_weight,
    down_weight,
):
    slot_count = features.shape[3]
    channels = features.shape[4]
    blocks = hilbert_dest.shape[3]
    halves = transposed_dest.shape[3]
    block = slot_count // blocks
    patch_blocks = PATCH // block
    count = block_count.reshape(1)
    vox_block = slot_voxel.reshape(blocks, 1, block)
    stream = features.reshape(slot_count, channels)
    dests = (hilbert_dest.reshape(blocks), transposed_dest.reshape(halves))
    axes = (("gy", "gz"), ("gx", "gz"))
    routes = []
    for layer, dest in enumerate(dests):
        owners = lax.axis_size(axes[layer][0]) * lax.axis_size(axes[layer][1])
        per_block = dest.shape[0] // blocks
        routes.append((owners, -(-dest.shape[0] // owners), patch_blocks * per_block, per_block, block // per_block))
    planes = 4
    if lax.axis_size("gx") == 2:
        index = lax.axis_index("gx")
        flags = jnp.stack([index == 1, index == 0]).astype(jnp.int32)
    else:
        flags = jnp.ones((2,), jnp.int32)
    faces_sent = 1 if lax.axis_size("gx") == 2 else 2
    placed = [(sds((CELLS, channels), BF16), "v"), (sds((faces_sent, VZ * VY, channels), BF16), "v")]
    placed += [(sds((2, PLANE, channels), BF16), "v")]
    placed += [(sds(conv_weight.shape[1:], BF16), "v")]
    weight_sems = pltpu.SemaphoreType.DMA((3,))
    rows_scratch = pltpu.VMEM((slot_count, channels), BF16)
    stream_scratch = pltpu.VMEM((slot_count, channels), F32)
    row_sems = pltpu.SemaphoreType.DMA((row_groups(slot_count),))
    pad_scratch = pltpu.VMEM((PX, VZ + 2, VY, channels), BF16)
    half_conv = CELLS // 2 * 27 * channels * channels * 2

    def route_scratch(layer):
        return [pltpu.SMEM((dests[layer].shape[0],), jnp.int32), pltpu.SMEM((routes[layer][0],), jnp.int32)]

    first = backs = None
    for layer in range(2):
        route = routes[layer]
        owners, capacity, per_owner, per_block, unit = route
        if layer == 0:
            own, xmsg, ymsg, weights = call(
                functools.partial(place_first_kernel, layer, block),
                placed,
                [(flags, "s"), (count, "s"), (vox_block, "v"), (stream, "v"), (conv_weight, "h")],
                [rows_scratch, weight_sems],
                "place0",
                44,
            )
        else:
            own, xmsg, ymsg, weights, stream = call(
                functools.partial(place_next_kernel, layer, routes[layer - 1]),
                placed + [(sds((slot_count, channels), F32), "v")],
                [(flags, "s"), (count, "s"), (dests[layer - 1], "s"), (vox_block, "v"), (first, "h")]
                + [(b, "v") for b in backs]
                + [(conv_weight, "h")],
                [rows_scratch, stream_scratch] + route_scratch(layer - 1) + [row_sems, weight_sems],
                "place1",
                44,
            )
        own = own.reshape(VX, VZ, VY, channels)
        xlo, xhi = exchange_x(xmsg.reshape(-1, VZ, VY, channels))
        middle = call(
            functools.partial(conv_middle_kernel, planes),
            [(sds((CELLS - 2 * planes * VZ * VY, channels), BF16), "v")],
            [(own, "v"), (weights, "v")],
            [pad_scratch],
            "conv_middle",
            24,
            half_conv,
        )
        zshape = (sds((PX, VY, channels), BF16), "v")
        faces = [
            (own, pl.BlockSpec((VX, None, VY, channels), lambda i, z=z: (0, z, 0, 0), pipeline_mode=pl.Buffered(1)))
            for z in (0, VZ - 1)
        ]
        zlow, zhigh = call(
            zface_kernel, [zshape, zshape], [(middle, "h"), (flags, "s")] + faces + [(xlo, "v"), (xhi, "v")], (), "zface", 8
        )
        zlo, zhi = up_down("gz", zlow, zhigh)
        ends = call(
            functools.partial(conv_ends_kernel, planes),
            [(sds((2 * planes * VZ * VY, channels), BF16), "v")],
            [(flags, "s"), (own, "v"), (xlo, "v"), (xhi, "v"), (weights, "v")],
            [pad_scratch],
            "conv_ends",
            24,
            half_conv,
        )
        yshape = (sds((PLANE, channels), BF16), "v")
        ylow, yhigh = call(
            yface_kernel,
            [yshape, yshape],
            [(ends, "h"), (flags, "s"), (ymsg, "v"), (xlo, "v"), (xhi, "v"), (zlo, "v"), (zhi, "v")],
            [pltpu.VMEM((896, channels), BF16)],
            "yface",
            8,
        )
        ylo, yhi = up_down("gy", ylow, yhigh)
        zc = call(
            conv_z_kernel,
            [(sds((2, VX, VY, channels), F32), "v")],
            [(zlo, "v"), (zhi, "v"), (weights, "v")],
            [],
            "conv_z",
            24,
            half_conv // 4,
        )
        slots = owners * capacity
        groups = blocks // next(g for g in (3, 2, 1) if blocks % g == 0)
        first, send = call(
            functools.partial(conv_finish_kernel, planes, route),
            [(sds((HELD * slot_count, channels), F32), "h"), (sds((slots, unit, channels), BF16), "v")],
            [(count, "s"), (dests[layer], "s"), (vox_block, "v"), (middle, "v"), (ends, "v"), (zc, "v")]
            + [(ylo, "v"), (yhi, "v"), (weights, "v"), (stream, "v")],
            [
                pltpu.VMEM((CELLS + 2 * VX * PZ, channels), BF16),
                stream_scratch,
            ]
            + route_scratch(layer)
            + [pltpu.SemaphoreType.DMA((groups,))],
            "conv_finish",
            24,
        )
        received = lax.all_to_all(send, axes[layer], split_axis=0, concat_axis=0, tiled=True)
        answers = owner_work(received, layer, qkv_weight, proj_weight, up_weight, down_weight)
        backs = [lax.all_to_all(a, axes[layer], split_axis=0, concat_axis=0, tiled=True) for a in answers]
    encoded = call(
        functools.partial(restore_kernel, routes[1]),
        [(sds((slot_count, channels), F32), "h")],
        [(count, "s"), (dests[1], "s"), (first, "h")] + [(b, "v") for b in backs],
        [stream_scratch, stream_scratch] + route_scratch(1) + [row_sems, row_sems],
        "restore",
        60,
    )
    return encoded.reshape(1, 1, 1, slot_count, channels)


def solution(mesh):
    in_specs = (
        P("gx", "gy", "gz", None, None),
        P("gx", "gy", "gz", None),
        P("gx", "gy", "gz"),
        P("gx", "gy", "gz", None),
        P("gx", "gy", "gz", None),
        P(),
        P(),
        P(),
        P(),
        P(),
    )
    out_specs = P("gx", "gy", "gz", None, None)
    return jax.shard_map(body, mesh=mesh, in_specs=in_specs, out_specs=out_specs, check_vma=False)
```

```python
import functools
import math

import jax
import jax.numpy as jnp
from jax import lax
from jax.experimental import pallas as pl
from jax.experimental.pallas import tpu as pltpu
from jax.sharding import PartitionSpec as P

HEADS = 16
PATCH = 1024
VX = 16
VY = 16
VZ = 8
PX = VX + 2
PZ = 16
CELLS = VX * VY * VZ
PLANE = PX * PZ
EPS = 1e-05
CLIP = 3e38
HELD = 24
F32 = jnp.float32
BF16 = jnp.bfloat16
SMEM = pltpu.MemorySpace.SMEM


def call(kernel, outs, ins, scratch=(), name=None, limit=24, flops=0):
    spaces = {"s": SMEM, "v": pltpu.MemorySpace.VMEM, "h": pltpu.MemorySpace.HBM}

    def spec(where):
        return pl.BlockSpec(memory_space=spaces[where]) if isinstance(where, str) else where

    windowed = any(not isinstance(where, str) for _, where in ins)
    result = pl.pallas_call(
        kernel,
        out_shape=tuple(shape for shape, _ in outs),
        grid=(1,) if windowed else (),
        in_specs=[spec(where) for _, where in ins],
        out_specs=tuple(spec(where) for _, where in outs),
        scratch_shapes=list(scratch),
        name=name,
        cost_estimate=pl.CostEstimate(flops=flops, transcendentals=0, bytes_accessed=1 << 20) if flops else None,
        compiler_params=pltpu.CompilerParams(vmem_limit_bytes=limit * 1024 * 1024),
    )(*(array for array, _ in ins))
    return result if len(outs) > 1 else result[0]


def row_groups(rows):
    return next(g for g in (5, 4, 3, 2, 1) if rows % (g * 128) == 0)


def group_copies(src_ref, dst_ref, sems):
    groups = sems.shape[0]
    size = min(src_ref.shape[0], dst_ref.shape[0]) // groups
    parts = [slice(g * size, (g + 1) * size) for g in range(groups)]
    return parts, [pltpu.make_async_copy(src_ref.at[p], dst_ref.at[p], sems.at[g]) for g, p in enumerate(parts)]


def weight_copies(layer, w_ref, dst_ref, sems):
    return [pltpu.make_async_copy(w_ref.at[layer, pl.ds(9 * da, 9)], dst_ref.at[pl.ds(9 * da, 9)], sems.at[da]) for da in range(3)]


def tap(w_ref, da, db, dc):
    return w_ref[9 * da + 3 * db + dc]


def sds(shape, dtype):
    return jax.ShapeDtypeStruct(shape, dtype)


def layer_norm(values):
    centred = values - jnp.mean(values, axis=-1, keepdims=True)
    variance = jnp.mean(centred * centred, axis=-1, keepdims=True)
    return centred * lax.rsqrt(variance + EPS)


def iota(shape, dim):
    return lax.broadcasted_iota(jnp.int32, shape, dim)


def cell_of(voxel):
    y = (voxel >> bits(VZ)) & (VY - 1)
    z = voxel & (VZ - 1)
    return ((voxel >> bits(VY * VZ)) << bits(VY * VZ)) | (z << bits(VY)) | y


def voxel_row(vox_ref):
    return jnp.concatenate([vox_ref[j] for j in range(vox_ref.shape[0])], axis=1)


def onehot(mask):
    return jnp.where(mask, 1.0, 0.0).astype(BF16)


def assign_slots(dest_ref, count_ref, slot_ref, used_ref, owners, capacity, per_owner, units_per_block):
    units = dest_ref.shape[0]

    def clear(o, c):
        used_ref[o] = 0
        return c

    lax.fori_loop(0, owners, clear, 0)

    def step(j, c):
        owner = jnp.maximum(dest_ref[j], 0) // per_owner
        rank = used_ref[owner]
        slot_ref[j] = jnp.minimum(owner * capacity + rank, owners * capacity - 1)
        used_ref[owner] = rank + 1
        return c

    lax.fori_loop(0, jnp.minimum(count_ref[0] * units_per_block, units), step, 0)


def place(rows_ref, ids, flags_ref, own_ref, xmsg_ref, ymsg_ref):
    slots = rows_ref.shape[0]
    tile = 256

    def one(t, c):
        r = iota((tile, slots), 0) + t * tile
        hot = onehot(r == ids)
        own_ref[pl.ds(pl.multiple_of(t * tile, tile), tile), :] = jnp.dot(
            hot, rows_ref[...], preferred_element_type=F32
        ).astype(BF16)
        return c

    lax.fori_loop(0, CELLS // tile, one, 0)
    face_rows = VZ * VY
    low, high = own_ref[0:face_rows], own_ref[CELLS - face_rows : CELLS]
    if xmsg_ref.shape[0] == 1:
        xmsg_ref[0] = jnp.where(flags_ref[1] > 0, high, low)
    else:
        xmsg_ref[0] = low
        xmsg_ref[1] = high
    for face in range(2):
        r = iota((PLANE, 1), 0)
        x = r // PZ - 1
        z = r % PZ - 1
        inside = (x >= 0) & (x < VX) & (z >= 0) & (z < VZ)
        cell = jnp.where(inside, (x * VZ + z) * VY + (VY - 1) * face, -2)
        hot = onehot(cell == ids)
        ymsg_ref[face] = jnp.dot(hot, rows_ref[...], preferred_element_type=F32).astype(BF16)


def place_first_kernel(
    layer, block, flags_ref, count_ref, vox_ref, feat_ref, w_in_ref, own_ref, xmsg_ref, ymsg_ref, w_ref, rows_ref, wsems
):
    slots = feat_ref.shape[0]
    weights = weight_copies(layer, w_in_ref, w_ref, wsems)
    for copy in weights:
        copy.start()
    rows_ref[...] = feat_ref[...].astype(BF16)
    live = iota((1, slots), 1) < count_ref[0] * block
    ids = jnp.where(live, cell_of(voxel_row(vox_ref)), -1)
    place(rows_ref, ids, flags_ref, own_ref, xmsg_ref, ymsg_ref)
    for copy in weights:
        copy.wait()


def restore_unit(u, unit, live_units, slot_ref, first_ref, backs):
    alive = u < live_units
    slot = jnp.where(alive, slot_ref[u], 0)
    part = unit // len(backs)
    for k, back_ref in enumerate(backs):
        rows = pl.ds(pl.multiple_of(u * unit + k * part, part), part)
        total = first_ref[rows, :].astype(F32) + back_ref[slot].astype(F32)
        yield rows, jnp.where(alive, total, 0.0)


def place_next_kernel(
    layer,
    route,
    flags_ref,
    count_ref,
    dest_ref,
    vox_ref,
    first_ref,
    back_a_ref,
    back_b_ref,
    w_in_ref,
    own_ref,
    xmsg_ref,
    ymsg_ref,
    w_ref,
    stream_ref,
    rows_ref,
    first_vmem,
    slot_ref,
    used_ref,
    sems,
    wsems,
):
    owners, capacity, per_owner, units_per_block, unit = route
    slots = first_vmem.shape[0]
    parts, copies = group_copies(first_ref, first_vmem, sems)
    weights = weight_copies(layer, w_in_ref, w_ref, wsems)
    for copy in copies + weights:
        copy.start()
    assign_slots(dest_ref, count_ref, slot_ref, used_ref, owners, capacity, per_owner, units_per_block)
    live_units = count_ref[0] * units_per_block
    per = slots // unit // len(parts)

    def one(u, c):
        for rows, value in restore_unit(u, unit, live_units, slot_ref, first_vmem, (back_a_ref, back_b_ref)):
            stream_ref[rows, :] = value
            rows_ref[rows, :] = value.astype(BF16)
        return c

    for g, copy in enumerate(copies):
        copy.wait()
        lax.fori_loop(g * per, (g + 1) * per, one, 0)
    live = iota((1, slots), 1) < live_units * unit
    ids = jnp.where(live, cell_of(voxel_row(vox_ref)), -1)
    place(rows_ref, ids, flags_ref, own_ref, xmsg_ref, ymsg_ref)
    for copy in weights:
        copy.wait()


def restore_kernel(
    route, count_ref, dest_ref, first_ref, back_a_ref, back_b_ref, out_ref, first_vmem, out_vmem, slot_ref, used_ref, sems, osems
):
    owners, capacity, per_owner, units_per_block, unit = route
    parts, copies = group_copies(first_ref, first_vmem, sems)
    _, sends = group_copies(out_vmem, out_ref, osems)
    for copy in copies:
        copy.start()
    assign_slots(dest_ref, count_ref, slot_ref, used_ref, owners, capacity, per_owner, units_per_block)
    live_units = count_ref[0] * units_per_block
    per = first_vmem.shape[0] // unit // len(parts)

    def one(u, c):
        for rows, value in restore_unit(u, unit, live_units, slot_ref, first_vmem, (back_a_ref, back_b_ref)):
            out_vmem[rows, :] = value
        return c

    for g, copy in enumerate(copies):
        copy.wait()
        lax.fori_loop(g * per, (g + 1) * per, one, 0)
        sends[g].start()
    for send in sends:
        send.wait()


def masked(flag, values):
    return jnp.where(flag > 0, values, jnp.zeros_like(values))


def zface_kernel(after_ref, flags_ref, bottom_ref, top_ref, lo_ref, hi_ref, out_lo_ref, out_hi_ref):
    for out_ref, z, face_ref in ((out_lo_ref, 0, bottom_ref), (out_hi_ref, VZ - 1, top_ref)):
        out_ref[0] = masked(flags_ref[0], lo_ref[z])
        out_ref[PX - 1] = masked(flags_ref[1], hi_ref[z])
        out_ref[1 : 1 + VX] = face_ref[...]


def yface_kernel(after_ref, flags_ref, ymsg_ref, xlo_ref, xhi_ref, zlo_ref, zhi_ref, out_lo_ref, out_hi_ref, src_ref):
    nx = VZ * VY
    nz = PX * VY
    src_ref[...] = jnp.zeros_like(src_ref)
    src_ref[0:nx] = masked(flags_ref[0], xlo_ref[...].reshape(nx, -1))
    src_ref[nx : 2 * nx] = masked(flags_ref[1], xhi_ref[...].reshape(nx, -1))
    src_ref[2 * nx : 2 * nx + nz] = zlo_ref[...].reshape(nz, -1)
    src_ref[2 * nx + nz : 2 * nx + 2 * nz] = zhi_ref[...].reshape(nz, -1)
    r = iota((PLANE, 1), 0)
    x = r // PZ
    z = r % PZ
    inner = (z >= 1) & (z <= VZ)
    for out_ref, face in ((out_lo_ref, 0), (out_hi_ref, 1)):
        y = (VY - 1) * face
        want = jnp.where(inner & (x == 0), (z - 1) * VY + y, -1)
        want = jnp.where(inner & (x == PX - 1), nx + (z - 1) * VY + y, want)
        want = jnp.where(z == 0, 2 * nx + x * VY + y, want)
        want = jnp.where(z == VZ + 1, 2 * nx + nz + x * VY + y, want)
        hot = onehot(iota((PLANE, src_ref.shape[0]), 1) == want)
        extra = jnp.dot(hot, src_ref[...], preferred_element_type=F32)
        out_ref[...] = (ymsg_ref[face].astype(F32) + extra).astype(BF16)


def conv_tiles(w_ref, out_ref, pad_ref, start, stride, count, planes):
    channels = pad_ref.shape[-1]
    rows = planes * VZ * VY

    def one(t, c):
        x0 = start + t * stride
        parts = []
        for da in range(3):
            for dc in range(3):
                window = pad_ref[pl.ds(x0 + da, planes), dc : dc + VZ]
                parts.append(window.reshape(rows, channels))
        lhs = jnp.concatenate(parts, axis=1)
        accs = []
        for db in range(3):
            rhs = jnp.concatenate([tap(w_ref, da, db, dc) for da in range(3) for dc in range(3)], axis=0)
            accs.append(jnp.dot(lhs, rhs, preferred_element_type=F32).reshape(planes * VZ, VY, channels))
        out_ref[pl.ds(pl.multiple_of(t * rows, rows), rows), :] = shift_sum(accs).reshape(rows, channels).astype(BF16)
        return c

    lax.fori_loop(0, count, one, 0)


def shift_sum(accs):
    y = iota(accs[0].shape, 1)
    low = jnp.where(y == 0, 0.0, pltpu.roll(accs[0], 1, 1))
    high = jnp.where(y == VY - 1, 0.0, pltpu.roll(accs[2], VY - 1, 1))
    return low + accs[1] + high


def clear_z(pad_ref, x):
    edge = jnp.zeros(pad_ref.shape[2:], BF16)
    pad_ref[x, 0] = edge
    pad_ref[x, VZ + 1] = edge


def conv_middle_kernel(planes, own_ref, w_ref, out_ref, pad_ref):
    for x in range(planes - 1, VX - planes + 1):
        clear_z(pad_ref, x + 1)
        pad_ref[x + 1, 1 : 1 + VZ] = own_ref[x]
    conv_tiles(w_ref, out_ref, pad_ref, planes, planes, VX // planes - 2, planes)


def conv_ends_kernel(planes, flags_ref, own_ref, xlo_ref, xhi_ref, w_ref, out_ref, pad_ref):
    for x in list(range(planes + 1)) + list(range(VX - planes - 1, VX)):
        clear_z(pad_ref, x + 1)
        pad_ref[x + 1, 1 : 1 + VZ] = own_ref[x]
    for x, halo_ref, k in ((0, xlo_ref, 0), (PX - 1, xhi_ref, 1)):
        clear_z(pad_ref, x)
        pad_ref[x, 1 : 1 + VZ] = masked(flags_ref[k], halo_ref[...])
    conv_tiles(w_ref, out_ref, pad_ref, 0, VX - planes, 2, planes)


def conv_z_kernel(zlo_ref, zhi_ref, w_ref, out_ref):
    channels = zlo_ref.shape[-1]
    for face, halo_ref in ((0, zlo_ref), (1, zhi_ref)):
        lhs = jnp.concatenate([halo_ref[da : da + VX].reshape(VX * VY, channels) for da in range(3)], axis=1)
        accs = []
        for db in range(3):
            rhs = jnp.concatenate([tap(w_ref, da, db, 2 * face) for da in range(3)], axis=0)
            accs.append(jnp.dot(lhs, rhs, preferred_element_type=F32).reshape(VX, VY, channels))
        out_ref[face] = shift_sum(accs)


def block_cells(vox_ref, j):
    block = vox_ref.shape[-1]
    cells = cell_of(vox_ref[j]).astype(F32)
    return jnp.transpose(jnp.broadcast_to(cells, (block, block))).astype(jnp.int32)


def bits(count):
    assert count & (count - 1) == 0
    return count.bit_length() - 1


def hot_row_groups(vox_ref):
    return next(g for g in (3, 2, 1) if vox_ref.shape[0] % g == 0)


def gather_kernel(planes, vox_ref, middle_ref, ends_ref, zc_ref, out_ref, table_ref):
    per_x = VZ * VY
    edge = planes * per_x
    table_ref[0:edge] = ends_ref[0:edge]
    table_ref[edge : CELLS - edge] = middle_ref[...]
    table_ref[CELLS - edge : CELLS] = ends_ref[edge:]
    for face, z in ((0, 0), (1, VZ - 1)):
        for x in range(VX):
            rows = slice(x * per_x + z * VY, x * per_x + (z + 1) * VY)
            table_ref[rows] = (table_ref[rows].astype(F32) + zc_ref[face, x]).astype(BF16)
    blocks, _, block = vox_ref.shape
    group = hot_row_groups(vox_ref)

    def hot_rows(j):
        cell = block_cells(vox_ref, j)
        lane = iota((block, block), 1)
        return jnp.concatenate([onehot(cell == lane + k * block) for k in range(CELLS // block)], axis=1)

    def one(g, c):
        hot = jnp.concatenate([hot_rows(g * group + i) for i in range(group)], axis=0)
        rows = pl.ds(pl.multiple_of(g * group * block, group * block), group * block)
        out_ref[rows, :] = jnp.dot(hot, table_ref[...], preferred_element_type=F32)
        return c

    lax.fori_loop(0, blocks // group, one, 0)


def conv_finish_kernel(
    route,
    count_ref,
    dest_ref,
    vox_ref,
    main_ref,
    lo_ref,
    hi_ref,
    w_ref,
    stream_ref,
    first_ref,
    send_ref,
    table_ref,
    first_vmem,
    slot_ref,
    used_ref,
    fsems,
):
    owners, capacity, per_owner, units_per_block, unit = route
    channels = main_ref.shape[-1]
    assign_slots(dest_ref, count_ref, slot_ref, used_ref, owners, capacity, per_owner, units_per_block)
    for s in range(owners * capacity):
        send_ref[s, 0:16] = jnp.full((16, channels), jnp.inf, BF16)
    plane_rows = VX * PZ
    for face, plane_ref in ((0, lo_ref), (1, hi_ref)):
        plane = plane_ref[...].reshape(PX, PZ, channels)
        wide = plane.astype(F32)
        shifted = [plane] + [pltpu.roll(wide, PZ - dc, 1).astype(BF16) for dc in (1, 2)]
        parts = [shifted[dc][da : da + VX].reshape(plane_rows, channels) for da in range(3) for dc in range(3)]
        rhs = jnp.concatenate([tap(w_ref, da, 2 * face, dc) for da in range(3) for dc in range(3)], axis=0)
        out = jnp.dot(jnp.concatenate(parts, axis=1), rhs, preferred_element_type=F32)
        table_ref[face * plane_rows : (face + 1) * plane_rows] = out.astype(BF16)
    blocks, _, block = vox_ref.shape
    group = hot_row_groups(vox_ref)
    live = count_ref[0]

    def hot_rows(j):
        cell = block_cells(vox_ref, j)
        y = cell & (VY - 1)
        spot = (cell >> bits(VY)) + (cell >> bits(VY * VZ)) * (PZ - VZ)
        lo = jnp.where(y == 0, spot, -1)
        hi = jnp.where(y == VY - 1, spot + plane_rows, -1)
        lane = iota((block, block), 1)
        pieces = []
        for k in range(2 * plane_rows // block):
            pieces.append(onehot((lo if k * block < plane_rows else hi) == lane + k * block))
        return jnp.concatenate(pieces, axis=1)

    def one(g, c):
        hot = jnp.concatenate([hot_rows(g * group + i) for i in range(group)], axis=0)
        rows = pl.ds(pl.multiple_of(g * group * block, group * block), group * block)
        gathered = main_ref[rows, :] + jnp.dot(hot, table_ref[...], preferred_element_type=F32)
        first = stream_ref[rows, :] + layer_norm(gathered)
        first_vmem[rows, :] = first.astype(BF16)
        pltpu.make_async_copy(first_vmem.at[rows], first_ref.at[rows], fsems.at[g]).start()
        packed = jnp.clip(first, -CLIP, CLIP).astype(BF16)
        for i in range(group):
            j = g * group + i

            @pl.when(j < live)
            def _():
                for k in range(units_per_block):
                    low = i * block + k * unit
                    send_ref[slot_ref[j * units_per_block + k]] = packed[low : low + unit]

        return c

    lax.fori_loop(0, blocks // group, one, 0)
    for g in range(blocks // group):
        rows = slice(g * group * block, (g + 1) * group * block)
        pltpu.make_async_copy(first_vmem.at[rows], first_ref.at[rows], fsems.at[g]).wait()


def attend_and_feed(x_ref, q_ref, kt_ref, va_ref, vb_ref, proj_ref, up_ref, down_ref, heads_ref, s0_ref, s1_ref, delta_ref, awaited):
    tile, channels = q_ref.shape
    half = channels // 2
    width = channels // HEADS
    scale = math.log2(math.e) / math.sqrt(width)
    group = iota((tile, half), 1) // width

    def score(h, side):
        cols = slice(side * half, (side + 1) * half)
        q = jnp.where(group == h, q_ref[:, cols].astype(F32), 0.0).astype(BF16)
        return jnp.dot(q, kt_ref[cols, :], preferred_element_type=F32)

    def combine(h, side, scores):
        cols = slice(side * half, (side + 1) * half)
        v_ref = (va_ref, vb_ref)[side]
        top = jnp.max(scores, axis=-1, keepdims=True)
        probs = jnp.exp2(((scores - top) * scale).astype(BF16))
        res = jnp.dot(probs, v_ref[...], preferred_element_type=F32)
        heads_ref[:, cols] = jnp.where(group == h, res[:, :half] / res[:, half:], heads_ref[:, cols])

    s0_ref[...] = score(0, 0)

    def head(h, c):
        s1_ref[...] = score(h, 1)
        combine(h, 0, s0_ref[...])
        s0_ref[...] = score(h + 1, 0)
        combine(h, 1, s1_ref[...])
        return c

    lax.fori_loop(0, half // width, head, 0)
    for copy in awaited:
        copy.wait()
    x = x_ref[0:tile, :].astype(F32)
    update = jnp.dot(heads_ref[...].astype(BF16), proj_ref[...], preferred_element_type=F32)
    normed = layer_norm(x + update).astype(BF16)
    hidden = jnp.dot(normed, up_ref[...], preferred_element_type=F32)
    hidden = (0.5 * hidden * (1.0 + lax.erf(hidden * (1.0 / math.sqrt(2.0))))).astype(BF16)
    delta_ref[...] = (update + jnp.dot(hidden, down_ref[...], preferred_element_type=F32)).astype(BF16)


def with_ones(v_ref, va_ref, vb_ref):
    rows, channels = v_ref.shape
    half = channels // 2
    ones = jnp.ones((rows, half), BF16)
    for side, ref in ((0, va_ref), (1, vb_ref)):
        ref[:, :half] = v_ref[:, side * half : (side + 1) * half]
        ref[:, half:] = ones


def answer_copies(pos_ref, delta_ref, out_ref, sems):
    slots, part, _ = out_ref.shape
    copies = []
    for s in range(slots):
        rows = pl.ds(pl.multiple_of(pos_ref[s] * part, part), part)
        copies.append(pltpu.make_async_copy(delta_ref.at[rows], out_ref.at[s], sems.at[s]))
        copies[-1].start()
    return copies


def owner_a_kernel(
    layer,
    recv_in_ref,
    qkv_in_ref,
    proj_in_ref,
    up_in_ref,
    down_in_ref,
    out_ref,
    xb_out_ref,
    qb_out_ref,
    kt_out_ref,
    v_out_ref,
    pos_ref,
    xa_ref,
    xb_ref,
    qa_ref,
    qb_ref,
    kt_ref,
    v_ref,
    va_ref,
    vb_ref,
    heads_ref,
    delta_ref,
    s0_ref,
    s1_ref,
    sems,
    osems,
    recv_ref,
    proj_ref,
    up_ref,
    down_ref,
    wsems,
    qkv_ref,
):
    pairs = ((qkv_in_ref, qkv_ref), (proj_in_ref, proj_ref), (up_in_ref, up_ref), (down_in_ref, down_ref))
    weights = [pltpu.make_async_copy(src.at[layer], dst, wsems.at[k]) for k, (src, dst) in enumerate(pairs)]
    arrival = pltpu.make_async_copy(recv_in_ref, recv_ref, osems.at[0])
    arrival.start()
    for copy in weights:
        copy.start()
    slots, unit, channels = recv_ref.shape
    part = unit // 2
    units = PATCH // unit
    tile = PATCH // 2
    pos = jnp.int32(0)
    arrival.wait()
    for s in range(slots):
        mark = jnp.max(recv_ref[s, 0:16, 0:128].astype(F32))
        pos_ref[s] = jnp.minimum(pos, units - 1)
        rows = pl.ds(pl.multiple_of(pos * part, part), part)
        xa_ref[rows, :] = recv_ref[s, :part]
        xb_ref[rows, :] = recv_ref[s, part:]
        pos = jnp.minimum(pos + jnp.where(mark > CLIP * 1.1, 0, 1), units)
    step = 256
    weights[0].wait()
    for c, (src_ref, dst_ref) in enumerate(((xa_ref, qa_ref), (xb_ref, qb_ref))):
        for t in range(tile // step):
            rows = slice(t * step, (t + 1) * step)
            both = slice(c * tile + t * step, c * tile + (t + 1) * step)
            normed = layer_norm(src_ref[rows, :].astype(F32)).astype(BF16)
            packed = jnp.dot(normed, qkv_ref[...], preferred_element_type=F32)
            dst_ref[rows, :] = packed[:, :channels].astype(BF16)
            kt_ref[:, both] = jnp.transpose(packed[:, channels : 2 * channels]).astype(BF16)
            v_ref[both, :] = packed[:, 2 * channels :].astype(BF16)
    pairs = ((xb_ref.at[0:tile], xb_out_ref), (qb_ref, qb_out_ref), (kt_ref, kt_out_ref), (v_ref, v_out_ref))
    handed = [pltpu.make_async_copy(src, dst, sems.at[k]) for k, (src, dst) in enumerate(pairs)]
    for copy in handed:
        copy.start()
    with_ones(v_ref, va_ref, vb_ref)
    attend_and_feed(
        xa_ref, qa_ref, kt_ref, va_ref, vb_ref, proj_ref, up_ref, down_ref, heads_ref, s0_ref, s1_ref, delta_ref, weights[1:]
    )
    for copy in handed + answer_copies(pos_ref, delta_ref, out_ref, osems):
        copy.wait()


def owner_b_kernel(
    layer,
    pos_ref,
    x_in_ref,
    q_in_ref,
    kt_in_ref,
    v_in_ref,
    proj_in_ref,
    up_in_ref,
    down_in_ref,
    out_ref,
    x_ref,
    q_ref,
    kt_ref,
    v_ref,
    va_ref,
    vb_ref,
    heads_ref,
    delta_ref,
    s0_ref,
    s1_ref,
    sems,
    osems,
    proj_ref,
    up_ref,
    down_ref,
    wsems,
):
    pairs = ((proj_in_ref, proj_ref), (up_in_ref, up_ref), (down_in_ref, down_ref))
    weights = [pltpu.make_async_copy(src.at[layer], dst, wsems.at[k]) for k, (src, dst) in enumerate(pairs)]
    pairs = ((q_in_ref, q_ref), (kt_in_ref, kt_ref), (v_in_ref, v_ref), (x_in_ref, x_ref))
    copies = [pltpu.make_async_copy(src, dst, sems.at[k]) for k, (src, dst) in enumerate(pairs)]
    for copy in copies + weights:
        copy.start()
    for copy in copies[:3]:
        copy.wait()
    with_ones(v_ref, va_ref, vb_ref)
    awaited = copies[3:] + weights
    attend_and_feed(
        x_ref, q_ref, kt_ref, va_ref, vb_ref, proj_ref, up_ref, down_ref, heads_ref, s0_ref, s1_ref, delta_ref, awaited
    )
    for copy in answer_copies(pos_ref, delta_ref, out_ref, osems):
        copy.wait()


def owner_work(received, layer, qkv_weight, proj_weight, up_weight, down_weight):
    slots, unit, channels = received.shape
    tile = PATCH // 2
    part = unit // 2
    arrays = (qkv_weight, proj_weight, up_weight, down_weight)
    weights = [(w, "h") for w in arrays]
    held_weights = [pltpu.VMEM(w.shape[1:], BF16) for w in arrays]
    half = pltpu.VMEM((tile, channels), BF16)
    whole = pltpu.VMEM((PATCH, channels), BF16)
    across = pltpu.VMEM((channels, PATCH), BF16)
    held = pltpu.VMEM((tile + part, channels), BF16)
    scores = pltpu.VMEM((tile, PATCH), F32)
    tail = [across, whole, whole, whole, pltpu.VMEM((tile, channels), F32), half, scores, scores]
    tail += [pltpu.SemaphoreType.DMA((4,)), pltpu.SemaphoreType.DMA((slots,))]
    answer = (sds((slots, part, channels), BF16), "h")
    rows = (sds((tile, channels), BF16), "h")
    out_a, xb, qb, kt, v, pos = call(
        functools.partial(owner_a_kernel, layer),
        [answer, rows, rows, (sds((channels, PATCH), BF16), "h"), (sds((PATCH, channels), BF16), "h")]
        + [(sds((slots,), jnp.int32), "s")],
        [(received, "h")] + weights,
        [held, held, half, half]
        + tail
        + [pltpu.VMEM(received.shape, BF16)]
        + held_weights[1:]
        + [pltpu.SemaphoreType.DMA((4,)), held_weights[0]],
        "owner_a",
        61,
        1 << 33,
    )
    out_b = call(
        functools.partial(owner_b_kernel, layer),
        [answer],
        [(pos, "s"), (xb, "h"), (qb, "h"), (kt, "h"), (v, "h")] + weights[1:],
        [half, half] + tail + held_weights[1:] + [pltpu.SemaphoreType.DMA((3,))],
        "owner_b",
        61,
        1 << 33,
    )
    return out_a, out_b


def up_down(axis, low_face, high_face):
    count = lax.axis_size(axis)
    ends = count - 1
    from_low = lax.ppermute(high_face, axis, [(i, (i + 1) % count) for i in range(ends)])
    from_high = lax.ppermute(low_face, axis, [((i + 1) % count, i) for i in range(ends)])
    return from_low, from_high


def exchange_x(faces):
    if faces.shape[0] == 1:
        got = lax.ppermute(faces, "gx", [(0, 1), (1, 0)]).reshape(faces.shape[1:])
        return got, got
    return up_down("gx", faces[0], faces[1])


def body(
    features,
    slot_voxel,
    block_count,
    hilbert_dest,
    transposed_dest,
    conv_weight,
    qkv_weight,
    proj_weight,
    up_weight,
    down_weight,
):
    slot_count = features.shape[3]
    channels = features.shape[4]
    blocks = hilbert_dest.shape[3]
    halves = transposed_dest.shape[3]
    block = slot_count // blocks
    patch_blocks = PATCH // block
    count = block_count.reshape(1)
    vox_block = slot_voxel.reshape(blocks, 1, block)
    stream = features.reshape(slot_count, channels)
    dests = (hilbert_dest.reshape(blocks), transposed_dest.reshape(halves))
    axes = (("gy", "gz"), ("gx", "gz"))
    routes = []
    for layer, dest in enumerate(dests):
        owners = lax.axis_size(axes[layer][0]) * lax.axis_size(axes[layer][1])
        per_block = dest.shape[0] // blocks
        routes.append((owners, -(-dest.shape[0] // owners), patch_blocks * per_block, per_block, block // per_block))
    planes = 4
    if lax.axis_size("gx") == 2:
        index = lax.axis_index("gx")
        flags = jnp.stack([index == 1, index == 0]).astype(jnp.int32)
    else:
        flags = jnp.ones((2,), jnp.int32)
    faces_sent = 1 if lax.axis_size("gx") == 2 else 2
    placed = [(sds((CELLS, channels), BF16), "v"), (sds((faces_sent, VZ * VY, channels), BF16), "v")]
    placed += [(sds((2, PLANE, channels), BF16), "v")]
    placed += [(sds(conv_weight.shape[1:], BF16), "v")]
    weight_sems = pltpu.SemaphoreType.DMA((3,))
    rows_scratch = pltpu.VMEM((slot_count, channels), BF16)
    stream_scratch = pltpu.VMEM((slot_count, channels), F32)
    row_sems = pltpu.SemaphoreType.DMA((row_groups(slot_count),))
    pad_scratch = pltpu.VMEM((PX, VZ + 2, VY, channels), BF16)
    half_conv = CELLS // 2 * 27 * channels * channels * 2

    def route_scratch(layer):
        return [pltpu.SMEM((dests[layer].shape[0],), jnp.int32), pltpu.SMEM((routes[layer][0],), jnp.int32)]

    first = backs = None
    for layer in range(2):
        route = routes[layer]
        owners, capacity, per_owner, per_block, unit = route
        if layer == 0:
            own, xmsg, ymsg, weights = call(
                functools.partial(place_first_kernel, layer, block),
                placed,
                [(flags, "s"), (count, "s"), (vox_block, "v"), (stream, "v"), (conv_weight, "h")],
                [rows_scratch, weight_sems],
                "place0",
                44,
            )
        else:
            own, xmsg, ymsg, weights, stream = call(
                functools.partial(place_next_kernel, layer, routes[layer - 1]),
                placed + [(sds((slot_count, channels), F32), "v")],
                [(flags, "s"), (count, "s"), (dests[layer - 1], "s"), (vox_block, "v"), (first, "h")]
                + [(b, "v") for b in backs]
                + [(conv_weight, "h")],
                [rows_scratch, rows_scratch] + route_scratch(layer - 1) + [row_sems, weight_sems],
                "place1",
                44,
            )
        own = own.reshape(VX, VZ, VY, channels)
        xlo, xhi = exchange_x(xmsg.reshape(-1, VZ, VY, channels))
        middle = call(
            functools.partial(conv_middle_kernel, planes),
            [(sds((CELLS - 2 * planes * VZ * VY, channels), BF16), "v")],
            [(own, "v"), (weights, "v")],
            [pad_scratch],
            "conv_middle",
            24,
            half_conv,
        )
        zshape = (sds((PX, VY, channels), BF16), "v")
        faces = [
            (own, pl.BlockSpec((VX, None, VY, channels), lambda i, z=z: (0, z, 0, 0), pipeline_mode=pl.Buffered(1)))
            for z in (0, VZ - 1)
        ]
        zlow, zhigh = call(
            zface_kernel, [zshape, zshape], [(middle, "h"), (flags, "s")] + faces + [(xlo, "v"), (xhi, "v")], (), "zface", 8
        )
        zlo, zhi = up_down("gz", zlow, zhigh)
        ends = call(
            functools.partial(conv_ends_kernel, planes),
            [(sds((2 * planes * VZ * VY, channels), BF16), "v")],
            [(flags, "s"), (own, "v"), (xlo, "v"), (xhi, "v"), (weights, "v")],
            [pad_scratch],
            "conv_ends",
            24,
            half_conv,
        )
        yshape = (sds((PLANE, channels), BF16), "v")
        ylow, yhigh = call(
            yface_kernel,
            [yshape, yshape],
            [(ends, "h"), (flags, "s"), (ymsg, "v"), (xlo, "v"), (xhi, "v"), (zlo, "v"), (zhi, "v")],
            [pltpu.VMEM((896, channels), BF16)],
            "yface",
            8,
        )
        ylo, yhi = up_down("gy", ylow, yhigh)
        zc = call(
            conv_z_kernel,
            [(sds((2, VX, VY, channels), F32), "v")],
            [(zlo, "v"), (zhi, "v"), (weights, "v")],
            [],
            "conv_z",
            24,
            half_conv // 4,
        )
        gathered = call(
            functools.partial(gather_kernel, planes),
            [(sds((slot_count, channels), F32), "v")],
            [(vox_block, "v"), (middle, "v"), (ends, "v"), (zc, "v")],
            [pltpu.VMEM((CELLS, channels), BF16)],
            "gather",
            24,
            half_conv // 2,
        )
        slots = owners * capacity
        groups = blocks // next(g for g in (3, 2, 1) if blocks % g == 0)
        first, send = call(
            functools.partial(conv_finish_kernel, route),
            [(sds((HELD * slot_count, channels), BF16), "h"), (sds((slots, unit, channels), BF16), "v")],
            [(count, "s"), (dests[layer], "s"), (vox_block, "v"), (gathered, "v")]
            + [(ylo, "v"), (yhi, "v"), (weights, "v"), (stream, "v")],
            [
                pltpu.VMEM((2 * VX * PZ, channels), BF16),
                rows_scratch,
            ]
            + route_scratch(layer)
            + [pltpu.SemaphoreType.DMA((groups,))],
            "conv_finish",
            24,
        )
        received = lax.all_to_all(send, axes[layer], split_axis=0, concat_axis=0, tiled=True)
        answers = owner_work(received, layer, qkv_weight, proj_weight, up_weight, down_weight)
        backs = [lax.all_to_all(a, axes[layer], split_axis=0, concat_axis=0, tiled=True) for a in answers]
    encoded = call(
        functools.partial(restore_kernel, routes[1]),
        [(sds((slot_count, channels), F32), "h")],
        [(count, "s"), (dests[1], "s"), (first, "h")] + [(b, "v") for b in backs],
        [rows_scratch, stream_scratch] + route_scratch(1) + [row_sems, row_sems],
        "restore",
        60,
    )
    return encoded.reshape(1, 1, 1, slot_count, channels)


def solution(mesh):
    in_specs = (
        P("gx", "gy", "gz", None, None),
        P("gx", "gy", "gz", None),
        P("gx", "gy", "gz"),
        P("gx", "gy", "gz", None),
        P("gx", "gy", "gz", None),
        P(),
        P(),
        P(),
        P(),
        P(),
    )
    out_specs = P("gx", "gy", "gz", None, None)
    return jax.shard_map(body, mesh=mesh, in_specs=in_specs, out_specs=out_specs, check_vma=False)
```

```python
import functools
import math

import jax
import jax.numpy as jnp
from jax import lax
from jax.experimental import pallas as pl
from jax.experimental.pallas import tpu as pltpu
from jax.sharding import PartitionSpec as P

HEADS = 16
PATCH = 1024
VX = 16
VY = 16
VZ = 8
PX = VX + 2
PZ = 16
CELLS = VX * VY * VZ
PLANE = PX * PZ
EPS = 1e-05
CLIP = 3e38
HELD = 24
F32 = jnp.float32
BF16 = jnp.bfloat16
SMEM = pltpu.MemorySpace.SMEM


def call(kernel, outs, ins, scratch=(), name=None, limit=24, flops=0):
    spaces = {"s": SMEM, "v": pltpu.MemorySpace.VMEM, "h": pltpu.MemorySpace.HBM}

    def spec(where):
        return pl.BlockSpec(memory_space=spaces[where]) if isinstance(where, str) else where

    windowed = any(not isinstance(where, str) for _, where in ins)
    result = pl.pallas_call(
        kernel,
        out_shape=tuple(shape for shape, _ in outs),
        grid=(1,) if windowed else (),
        in_specs=[spec(where) for _, where in ins],
        out_specs=tuple(spec(where) for _, where in outs),
        scratch_shapes=list(scratch),
        name=name,
        cost_estimate=pl.CostEstimate(flops=flops, transcendentals=0, bytes_accessed=1 << 20) if flops else None,
        compiler_params=pltpu.CompilerParams(vmem_limit_bytes=limit * 1024 * 1024),
    )(*(array for array, _ in ins))
    return result if len(outs) > 1 else result[0]


def row_groups(rows):
    return next(g for g in (5, 4, 3, 2, 1) if rows % (g * 128) == 0)


def group_copies(src_ref, dst_ref, sems):
    groups = sems.shape[0]
    size = min(src_ref.shape[0], dst_ref.shape[0]) // groups
    parts = [slice(g * size, (g + 1) * size) for g in range(groups)]
    return parts, [pltpu.make_async_copy(src_ref.at[p], dst_ref.at[p], sems.at[g]) for g, p in enumerate(parts)]


def weight_copies(layer, w_ref, dst_ref, sems):
    return [pltpu.make_async_copy(w_ref.at[layer, pl.ds(9 * da, 9)], dst_ref.at[pl.ds(9 * da, 9)], sems.at[da]) for da in range(3)]


def tap(w_ref, da, db, dc):
    return w_ref[9 * da + 3 * db + dc]


def sds(shape, dtype):
    return jax.ShapeDtypeStruct(shape, dtype)


def layer_norm(values):
    centred = values - jnp.mean(values, axis=-1, keepdims=True)
    variance = jnp.mean(centred * centred, axis=-1, keepdims=True)
    return centred * lax.rsqrt(variance + EPS)


def iota(shape, dim):
    return lax.broadcasted_iota(jnp.int32, shape, dim)


def cell_of(voxel):
    y = (voxel >> bits(VZ)) & (VY - 1)
    z = voxel & (VZ - 1)
    return ((voxel >> bits(VY * VZ)) << bits(VY * VZ)) | (z << bits(VY)) | y


def voxel_row(vox_ref):
    return jnp.concatenate([vox_ref[j] for j in range(vox_ref.shape[0])], axis=1)


def onehot(mask):
    return jnp.where(mask, 1.0, 0.0).astype(BF16)


def assign_slots(dest_ref, count_ref, slot_ref, used_ref, owners, capacity, per_owner, units_per_block):
    units = dest_ref.shape[0]

    def clear(o, c):
        used_ref[o] = 0
        return c

    lax.fori_loop(0, owners, clear, 0)

    def step(j, c):
        owner = jnp.maximum(dest_ref[j], 0) // per_owner
        rank = used_ref[owner]
        slot_ref[j] = jnp.minimum(owner * capacity + rank, owners * capacity - 1)
        used_ref[owner] = rank + 1
        return c

    lax.fori_loop(0, jnp.minimum(count_ref[0] * units_per_block, units), step, 0)


def place(rows_ref, ids, flags_ref, own_ref, xmsg_ref, ymsg_ref):
    slots = rows_ref.shape[0]
    tile = 256

    def one(t, c):
        r = iota((tile, slots), 0) + t * tile
        hot = onehot(r == ids)
        own_ref[pl.ds(pl.multiple_of(t * tile, tile), tile), :] = jnp.dot(
            hot, rows_ref[...], preferred_element_type=F32
        ).astype(BF16)
        return c

    lax.fori_loop(0, CELLS // tile, one, 0)
    face_rows = VZ * VY
    low, high = own_ref[0:face_rows], own_ref[CELLS - face_rows : CELLS]
    if xmsg_ref.shape[0] == 1:
        xmsg_ref[0] = jnp.where(flags_ref[1] > 0, high, low)
    else:
        xmsg_ref[0] = low
        xmsg_ref[1] = high
    for face in range(2):
        r = iota((PLANE, 1), 0)
        x = r // PZ - 1
        z = r % PZ - 1
        inside = (x >= 0) & (x < VX) & (z >= 0) & (z < VZ)
        cell = jnp.where(inside, (x * VZ + z) * VY + (VY - 1) * face, -2)
        hot = onehot(cell == ids)
        ymsg_ref[face] = jnp.dot(hot, rows_ref[...], preferred_element_type=F32).astype(BF16)


def place_first_kernel(
    layer, block, flags_ref, count_ref, vox_ref, feat_ref, w_in_ref, own_ref, xmsg_ref, ymsg_ref, w_ref, rows_ref, wsems
):
    slots = feat_ref.shape[0]
    weights = weight_copies(layer, w_in_ref, w_ref, wsems)
    for copy in weights:
        copy.start()
    rows_ref[...] = feat_ref[...].astype(BF16)
    live = iota((1, slots), 1) < count_ref[0] * block
    ids = jnp.where(live, cell_of(voxel_row(vox_ref)), -1)
    place(rows_ref, ids, flags_ref, own_ref, xmsg_ref, ymsg_ref)
    for copy in weights:
        copy.wait()


def restore_unit(u, unit, live_units, slot_ref, first_ref, backs):
    alive = u < live_units
    slot = jnp.where(alive, slot_ref[u], 0)
    part = unit // len(backs)
    for k, back_ref in enumerate(backs):
        rows = pl.ds(pl.multiple_of(u * unit + k * part, part), part)
        total = first_ref[rows, :].astype(F32) + back_ref[slot].astype(F32)
        yield rows, jnp.where(alive, total, 0.0)


def place_next_kernel(
    layer,
    route,
    flags_ref,
    count_ref,
    dest_ref,
    vox_ref,
    first_ref,
    back_a_ref,
    back_b_ref,
    w_in_ref,
    own_ref,
    xmsg_ref,
    ymsg_ref,
    w_ref,
    stream_ref,
    rows_ref,
    first_vmem,
    slot_ref,
    used_ref,
    sems,
    wsems,
):
    owners, capacity, per_owner, units_per_block, unit = route
    slots = first_vmem.shape[0]
    parts, copies = group_copies(first_ref, first_vmem, sems)
    weights = weight_copies(layer, w_in_ref, w_ref, wsems)
    for copy in copies + weights:
        copy.start()
    assign_slots(dest_ref, count_ref, slot_ref, used_ref, owners, capacity, per_owner, units_per_block)
    live_units = count_ref[0] * units_per_block
    per = slots // unit // len(parts)

    def one(u, c):
        for rows, value in restore_unit(u, unit, live_units, slot_ref, first_vmem, (back_a_ref, back_b_ref)):
            stream_ref[rows, :] = value
            rows_ref[rows, :] = value.astype(BF16)
        return c

    for g, copy in enumerate(copies):
        copy.wait()
        lax.fori_loop(g * per, (g + 1) * per, one, 0)
    live = iota((1, slots), 1) < live_units * unit
    ids = jnp.where(live, cell_of(voxel_row(vox_ref)), -1)
    place(rows_ref, ids, flags_ref, own_ref, xmsg_ref, ymsg_ref)
    for copy in weights:
        copy.wait()


def restore_kernel(
    route, count_ref, dest_ref, first_ref, back_a_ref, back_b_ref, out_ref, first_vmem, out_vmem, slot_ref, used_ref, sems, osems
):
    owners, capacity, per_owner, units_per_block, unit = route
    parts, copies = group_copies(first_ref, first_vmem, sems)
    _, sends = group_copies(out_vmem, out_ref, osems)
    for copy in copies:
        copy.start()
    assign_slots(dest_ref, count_ref, slot_ref, used_ref, owners, capacity, per_owner, units_per_block)
    live_units = count_ref[0] * units_per_block
    per = first_vmem.shape[0] // unit // len(parts)

    def one(u, c):
        for rows, value in restore_unit(u, unit, live_units, slot_ref, first_vmem, (back_a_ref, back_b_ref)):
            out_vmem[rows, :] = value
        return c

    for g, copy in enumerate(copies):
        copy.wait()
        lax.fori_loop(g * per, (g + 1) * per, one, 0)
        sends[g].start()
    for send in sends:
        send.wait()


def masked(flag, values):
    return jnp.where(flag > 0, values, jnp.zeros_like(values))


def zface_kernel(after_ref, flags_ref, bottom_ref, top_ref, lo_ref, hi_ref, out_lo_ref, out_hi_ref):
    for out_ref, z, face_ref in ((out_lo_ref, 0, bottom_ref), (out_hi_ref, VZ - 1, top_ref)):
        out_ref[0] = masked(flags_ref[0], lo_ref[z])
        out_ref[PX - 1] = masked(flags_ref[1], hi_ref[z])
        out_ref[1 : 1 + VX] = face_ref[...]


def yface_kernel(after_ref, flags_ref, ymsg_ref, xlo_ref, xhi_ref, zlo_ref, zhi_ref, out_lo_ref, out_hi_ref, src_ref):
    nx = VZ * VY
    nz = PX * VY
    src_ref[...] = jnp.zeros_like(src_ref)
    src_ref[0:nx] = masked(flags_ref[0], xlo_ref[...].reshape(nx, -1))
    src_ref[nx : 2 * nx] = masked(flags_ref[1], xhi_ref[...].reshape(nx, -1))
    src_ref[2 * nx : 2 * nx + nz] = zlo_ref[...].reshape(nz, -1)
    src_ref[2 * nx + nz : 2 * nx + 2 * nz] = zhi_ref[...].reshape(nz, -1)
    r = iota((PLANE, 1), 0)
    x = r // PZ
    z = r % PZ
    inner = (z >= 1) & (z <= VZ)
    for out_ref, face in ((out_lo_ref, 0), (out_hi_ref, 1)):
        y = (VY - 1) * face
        want = jnp.where(inner & (x == 0), (z - 1) * VY + y, -1)
        want = jnp.where(inner & (x == PX - 1), nx + (z - 1) * VY + y, want)
        want = jnp.where(z == 0, 2 * nx + x * VY + y, want)
        want = jnp.where(z == VZ + 1, 2 * nx + nz + x * VY + y, want)
        hot = onehot(iota((PLANE, src_ref.shape[0]), 1) == want)
        extra = jnp.dot(hot, src_ref[...], preferred_element_type=F32)
        out_ref[...] = (ymsg_ref[face].astype(F32) + extra).astype(BF16)


def conv_tiles(w_ref, out_ref, pad_ref, start, stride, count, planes):
    channels = pad_ref.shape[-1]
    rows = planes * VZ * VY

    def one(t, c):
        x0 = start + t * stride
        parts = []
        for da in range(3):
            for dc in range(3):
                window = pad_ref[pl.ds(x0 + da, planes), dc : dc + VZ]
                parts.append(window.reshape(rows, channels))
        lhs = jnp.concatenate(parts, axis=1)
        accs = []
        for db in range(3):
            rhs = jnp.concatenate([tap(w_ref, da, db, dc) for da in range(3) for dc in range(3)], axis=0)
            accs.append(jnp.dot(lhs, rhs, preferred_element_type=F32).reshape(planes * VZ, VY, channels))
        out_ref[pl.ds(pl.multiple_of(t * rows, rows), rows), :] = shift_sum(accs).reshape(rows, channels).astype(BF16)
        return c

    lax.fori_loop(0, count, one, 0)


def shift_sum(accs):
    y = iota(accs[0].shape, 1)
    low = jnp.where(y == 0, 0.0, pltpu.roll(accs[0], 1, 1))
    high = jnp.where(y == VY - 1, 0.0, pltpu.roll(accs[2], VY - 1, 1))
    return low + accs[1] + high


def clear_z(pad_ref, x):
    edge = jnp.zeros(pad_ref.shape[2:], BF16)
    pad_ref[x, 0] = edge
    pad_ref[x, VZ + 1] = edge


def conv_middle_kernel(planes, own_ref, w_ref, out_ref, pad_ref):
    for x in range(planes - 1, VX - planes + 1):
        clear_z(pad_ref, x + 1)
        pad_ref[x + 1, 1 : 1 + VZ] = own_ref[x]
    conv_tiles(w_ref, out_ref, pad_ref, planes, planes, VX // planes - 2, planes)


def conv_ends_kernel(planes, flags_ref, own_ref, xlo_ref, xhi_ref, w_ref, out_ref, pad_ref):
    for x in list(range(planes + 1)) + list(range(VX - planes - 1, VX)):
        clear_z(pad_ref, x + 1)
        pad_ref[x + 1, 1 : 1 + VZ] = own_ref[x]
    for x, halo_ref, k in ((0, xlo_ref, 0), (PX - 1, xhi_ref, 1)):
        clear_z(pad_ref, x)
        pad_ref[x, 1 : 1 + VZ] = masked(flags_ref[k], halo_ref[...])
    conv_tiles(w_ref, out_ref, pad_ref, 0, VX - planes, 2, planes)


def conv_z_kernel(zlo_ref, zhi_ref, w_ref, out_ref):
    channels = zlo_ref.shape[-1]
    for face, halo_ref in ((0, zlo_ref), (1, zhi_ref)):
        lhs = jnp.concatenate([halo_ref[da : da + VX].reshape(VX * VY, channels) for da in range(3)], axis=1)
        accs = []
        for db in range(3):
            rhs = jnp.concatenate([tap(w_ref, da, db, 2 * face) for da in range(3)], axis=0)
            accs.append(jnp.dot(lhs, rhs, preferred_element_type=F32).reshape(VX, VY, channels))
        out_ref[face] = shift_sum(accs)


def block_cells(vox_ref, j):
    block = vox_ref.shape[-1]
    cells = cell_of(vox_ref[j]).astype(F32)
    return jnp.transpose(jnp.broadcast_to(cells, (block, block))).astype(jnp.int32)


def bits(count):
    assert count & (count - 1) == 0
    return count.bit_length() - 1


def hot_row_groups(vox_ref):
    return next(g for g in (3, 2, 1) if vox_ref.shape[0] % g == 0)


def gather_kernel(planes, vox_ref, middle_ref, ends_ref, zc_ref, out_ref, table_ref):
    per_x = VZ * VY
    edge = planes * per_x
    table_ref[0:edge] = ends_ref[0:edge]
    table_ref[edge : CELLS - edge] = middle_ref[...]
    table_ref[CELLS - edge : CELLS] = ends_ref[edge:]
    for face, z in ((0, 0), (1, VZ - 1)):
        for x in range(VX):
            rows = slice(x * per_x + z * VY, x * per_x + (z + 1) * VY)
            table_ref[rows] = (table_ref[rows].astype(F32) + zc_ref[face, x]).astype(BF16)
    blocks, _, block = vox_ref.shape
    group = hot_row_groups(vox_ref)

    def hot_rows(j):
        cell = block_cells(vox_ref, j)
        lane = iota((block, block), 1)
        return jnp.concatenate([onehot(cell == lane + k * block) for k in range(CELLS // block)], axis=1)

    def one(g, c):
        hot = jnp.concatenate([hot_rows(g * group + i) for i in range(group)], axis=0)
        rows = pl.ds(pl.multiple_of(g * group * block, group * block), group * block)
        out_ref[rows, :] = jnp.dot(hot, table_ref[...], preferred_element_type=F32)
        return c

    lax.fori_loop(0, blocks // group, one, 0)


def conv_finish_kernel(
    route,
    count_ref,
    dest_ref,
    vox_ref,
    main_ref,
    lo_ref,
    hi_ref,
    w_ref,
    stream_ref,
    first_ref,
    send_ref,
    table_ref,
    first_vmem,
    slot_ref,
    used_ref,
    fsems,
):
    owners, capacity, per_owner, units_per_block, unit = route
    channels = main_ref.shape[-1]
    assign_slots(dest_ref, count_ref, slot_ref, used_ref, owners, capacity, per_owner, units_per_block)
    for s in range(owners * capacity):
        send_ref[s, 0:16] = jnp.full((16, channels), jnp.inf, BF16)
    plane_rows = VX * PZ
    for face, plane_ref in ((0, lo_ref), (1, hi_ref)):
        plane = plane_ref[...].reshape(PX, PZ, channels)
        wide = plane.astype(F32)
        shifted = [plane] + [pltpu.roll(wide, PZ - dc, 1).astype(BF16) for dc in (1, 2)]
        parts = [shifted[dc][da : da + VX].reshape(plane_rows, channels) for da in range(3) for dc in range(3)]
        rhs = jnp.concatenate([tap(w_ref, da, 2 * face, dc) for da in range(3) for dc in range(3)], axis=0)
        out = jnp.dot(jnp.concatenate(parts, axis=1), rhs, preferred_element_type=F32)
        table_ref[face * plane_rows : (face + 1) * plane_rows] = out.astype(BF16)
    blocks, _, block = vox_ref.shape
    group = hot_row_groups(vox_ref)
    live = count_ref[0]

    def hot_rows(j):
        cell = block_cells(vox_ref, j)
        y = cell & (VY - 1)
        spot = (cell >> bits(VY)) + (cell >> bits(VY * VZ)) * (PZ - VZ)
        lo = jnp.where(y == 0, spot, -1)
        hi = jnp.where(y == VY - 1, spot + plane_rows, -1)
        lane = iota((block, block), 1)
        pieces = []
        for k in range(2 * plane_rows // block):
            pieces.append(onehot((lo if k * block < plane_rows else hi) == lane + k * block))
        return jnp.concatenate(pieces, axis=1)

    def one(g, c):
        hot = jnp.concatenate([hot_rows(g * group + i) for i in range(group)], axis=0)
        rows = pl.ds(pl.multiple_of(g * group * block, group * block), group * block)
        gathered = main_ref[rows, :] + jnp.dot(hot, table_ref[...], preferred_element_type=F32)
        first = stream_ref[rows, :] + layer_norm(gathered)
        first_vmem[rows, :] = first.astype(BF16)
        pltpu.make_async_copy(first_vmem.at[rows], first_ref.at[rows], fsems.at[g]).start()
        packed = jnp.clip(first, -CLIP, CLIP).astype(BF16)
        for i in range(group):
            j = g * group + i

            @pl.when(j < live)
            def _():
                for k in range(units_per_block):
                    low = i * block + k * unit
                    send_ref[slot_ref[j * units_per_block + k]] = packed[low : low + unit]

        return c

    lax.fori_loop(0, blocks // group, one, 0)
    for g in range(blocks // group):
        rows = slice(g * group * block, (g + 1) * group * block)
        pltpu.make_async_copy(first_vmem.at[rows], first_ref.at[rows], fsems.at[g]).wait()


def attend_and_feed(x_ref, q_ref, kt_ref, v_ref, proj_ref, up_ref, down_ref, heads_ref, s0_ref, s1_ref, delta_ref, awaited):
    tile, channels = q_ref.shape
    half = channels // 2
    width = channels // HEADS
    scale = math.log2(math.e) / math.sqrt(width)
    group = iota((tile, half), 1) // width
    ones = jnp.ones((PATCH, half), BF16)

    def score(h, side):
        cols = slice(side * half, (side + 1) * half)
        q = jnp.where(group == h, q_ref[:, cols].astype(F32), 0.0).astype(BF16)
        return jnp.dot(q, kt_ref[cols, :], preferred_element_type=F32)

    def combine(h, side, scores):
        cols = slice(side * half, (side + 1) * half)
        rhs = jnp.concatenate([v_ref[:, cols], ones], axis=1)
        top = jnp.max(scores, axis=-1, keepdims=True)
        probs = jnp.exp2(((scores - top) * scale).astype(BF16))
        res = jnp.dot(probs, rhs, preferred_element_type=F32)
        heads_ref[:, cols] = jnp.where(group == h, res[:, :half] / res[:, half:], heads_ref[:, cols])

    s0_ref[...] = score(0, 0)

    def head(h, c):
        s1_ref[...] = score(h, 1)
        combine(h, 0, s0_ref[...])
        s0_ref[...] = score(h + 1, 0)
        combine(h, 1, s1_ref[...])
        return c

    lax.fori_loop(0, half // width, head, 0)
    for copy in awaited:
        copy.wait()
    x = x_ref[0:tile, :].astype(F32)
    update = jnp.dot(heads_ref[...].astype(BF16), proj_ref[...], preferred_element_type=F32)
    normed = layer_norm(x + update).astype(BF16)
    hidden = jnp.dot(normed, up_ref[...], preferred_element_type=F32)
    hidden = (0.5 * hidden * (1.0 + lax.erf(hidden * (1.0 / math.sqrt(2.0))))).astype(BF16)
    delta_ref[...] = (update + jnp.dot(hidden, down_ref[...], preferred_element_type=F32)).astype(BF16)


def answer_copies(pos_ref, delta_ref, out_ref, sems):
    slots, part, _ = out_ref.shape
    copies = []
    for s in range(slots):
        rows = pl.ds(pl.multiple_of(pos_ref[s] * part, part), part)
        copies.append(pltpu.make_async_copy(delta_ref.at[rows], out_ref.at[s], sems.at[s]))
        copies[-1].start()
    return copies


def owner_a_kernel(
    layer,
    recv_in_ref,
    qkv_in_ref,
    proj_in_ref,
    up_in_ref,
    down_in_ref,
    out_ref,
    xb_out_ref,
    qb_out_ref,
    kt_out_ref,
    v_out_ref,
    pos_ref,
    xa_ref,
    xb_ref,
    qa_ref,
    qb_ref,
    kt_ref,
    v_ref,
    heads_ref,
    delta_ref,
    s0_ref,
    s1_ref,
    sems,
    osems,
    recv_ref,
    proj_ref,
    up_ref,
    down_ref,
    wsems,
    qkv_ref,
):
    pairs = ((qkv_in_ref, qkv_ref), (proj_in_ref, proj_ref), (up_in_ref, up_ref), (down_in_ref, down_ref))
    weights = [pltpu.make_async_copy(src.at[layer], dst, wsems.at[k]) for k, (src, dst) in enumerate(pairs)]
    arrival = pltpu.make_async_copy(recv_in_ref, recv_ref, osems.at[0])
    arrival.start()
    for copy in weights:
        copy.start()
    slots, unit, channels = recv_ref.shape
    part = unit // 2
    units = PATCH // unit
    tile = PATCH // 2
    pos = jnp.int32(0)
    arrival.wait()
    for s in range(slots):
        mark = jnp.max(recv_ref[s, 0:16, 0:128].astype(F32))
        pos_ref[s] = jnp.minimum(pos, units - 1)
        rows = pl.ds(pl.multiple_of(pos * part, part), part)
        xa_ref[rows, :] = recv_ref[s, :part]
        xb_ref[rows, :] = recv_ref[s, part:]
        pos = jnp.minimum(pos + jnp.where(mark > CLIP * 1.1, 0, 1), units)
    step = 256
    weights[0].wait()
    for c, (src_ref, dst_ref) in enumerate(((xa_ref, qa_ref), (xb_ref, qb_ref))):
        for t in range(tile // step):
            rows = slice(t * step, (t + 1) * step)
            both = slice(c * tile + t * step, c * tile + (t + 1) * step)
            normed = layer_norm(src_ref[rows, :].astype(F32)).astype(BF16)
            packed = jnp.dot(normed, qkv_ref[...], preferred_element_type=F32)
            dst_ref[rows, :] = packed[:, :channels].astype(BF16)
            kt_ref[:, both] = jnp.transpose(packed[:, channels : 2 * channels]).astype(BF16)
            v_ref[both, :] = packed[:, 2 * channels :].astype(BF16)
    pairs = ((xb_ref.at[0:tile], xb_out_ref), (qb_ref, qb_out_ref), (kt_ref, kt_out_ref), (v_ref, v_out_ref))
    handed = [pltpu.make_async_copy(src, dst, sems.at[k]) for k, (src, dst) in enumerate(pairs)]
    for copy in handed:
        copy.start()
    attend_and_feed(
        xa_ref, qa_ref, kt_ref, v_ref, proj_ref, up_ref, down_ref, heads_ref, s0_ref, s1_ref, delta_ref, weights[1:]
    )
    for copy in handed + answer_copies(pos_ref, delta_ref, out_ref, osems):
        copy.wait()


def owner_b_kernel(
    layer,
    pos_ref,
    x_in_ref,
    q_in_ref,
    kt_in_ref,
    v_in_ref,
    proj_in_ref,
    up_in_ref,
    down_in_ref,
    out_ref,
    x_ref,
    q_ref,
    kt_ref,
    v_ref,
    heads_ref,
    delta_ref,
    s0_ref,
    s1_ref,
    sems,
    osems,
    proj_ref,
    up_ref,
    down_ref,
    wsems,
):
    pairs = ((proj_in_ref, proj_ref), (up_in_ref, up_ref), (down_in_ref, down_ref))
    weights = [pltpu.make_async_copy(src.at[layer], dst, wsems.at[k]) for k, (src, dst) in enumerate(pairs)]
    pairs = ((q_in_ref, q_ref), (kt_in_ref, kt_ref), (v_in_ref, v_ref), (x_in_ref, x_ref))
    copies = [pltpu.make_async_copy(src, dst, sems.at[k]) for k, (src, dst) in enumerate(pairs)]
    for copy in copies + weights:
        copy.start()
    for copy in copies[:3]:
        copy.wait()
    awaited = copies[3:] + weights
    attend_and_feed(
        x_ref, q_ref, kt_ref, v_ref, proj_ref, up_ref, down_ref, heads_ref, s0_ref, s1_ref, delta_ref, awaited
    )
    for copy in answer_copies(pos_ref, delta_ref, out_ref, osems):
        copy.wait()


def owner_work(received, layer, qkv_weight, proj_weight, up_weight, down_weight):
    slots, unit, channels = received.shape
    tile = PATCH // 2
    part = unit // 2
    arrays = (qkv_weight, proj_weight, up_weight, down_weight)
    weights = [(w, "h") for w in arrays]
    held_weights = [pltpu.VMEM(w.shape[1:], BF16) for w in arrays]
    half = pltpu.VMEM((tile, channels), BF16)
    whole = pltpu.VMEM((PATCH, channels), BF16)
    across = pltpu.VMEM((channels, PATCH), BF16)
    held = pltpu.VMEM((tile + part, channels), BF16)
    scores = pltpu.VMEM((tile, PATCH), F32)
    tail = [across, whole, pltpu.VMEM((tile, channels), F32), half, scores, scores]
    tail += [pltpu.SemaphoreType.DMA((4,)), pltpu.SemaphoreType.DMA((slots,))]
    answer = (sds((slots, part, channels), BF16), "h")
    rows = (sds((tile, channels), BF16), "h")
    out_a, xb, qb, kt, v, pos = call(
        functools.partial(owner_a_kernel, layer),
        [answer, rows, rows, (sds((channels, PATCH), BF16), "h"), (sds((PATCH, channels), BF16), "h")]
        + [(sds((slots,), jnp.int32), "s")],
        [(received, "h")] + weights,
        [held, held, half, half]
        + tail
        + [pltpu.VMEM(received.shape, BF16)]
        + held_weights[1:]
        + [pltpu.SemaphoreType.DMA((4,)), held_weights[0]],
        "owner_a",
        61,
        1 << 33,
    )
    out_b = call(
        functools.partial(owner_b_kernel, layer),
        [answer],
        [(pos, "s"), (xb, "h"), (qb, "h"), (kt, "h"), (v, "h")] + weights[1:],
        [half, half] + tail + held_weights[1:] + [pltpu.SemaphoreType.DMA((3,))],
        "owner_b",
        61,
        1 << 33,
    )
    return out_a, out_b


def up_down(axis, low_face, high_face):
    count = lax.axis_size(axis)
    ends = count - 1
    from_low = lax.ppermute(high_face, axis, [(i, (i + 1) % count) for i in range(ends)])
    from_high = lax.ppermute(low_face, axis, [((i + 1) % count, i) for i in range(ends)])
    return from_low, from_high


def exchange_x(faces):
    if faces.shape[0] == 1:
        got = lax.ppermute(faces, "gx", [(0, 1), (1, 0)]).reshape(faces.shape[1:])
        return got, got
    return up_down("gx", faces[0], faces[1])


def body(
    features,
    slot_voxel,
    block_count,
    hilbert_dest,
    transposed_dest,
    conv_weight,
    qkv_weight,
    proj_weight,
    up_weight,
    down_weight,
):
    slot_count = features.shape[3]
    channels = features.shape[4]
    blocks = hilbert_dest.shape[3]
    halves = transposed_dest.shape[3]
    block = slot_count // blocks
    patch_blocks = PATCH // block
    count = block_count.reshape(1)
    vox_block = slot_voxel.reshape(blocks, 1, block)
    stream = features.reshape(slot_count, channels)
    dests = (hilbert_dest.reshape(blocks), transposed_dest.reshape(halves))
    axes = (("gy", "gz"), ("gx", "gz"))
    routes = []
    for layer, dest in enumerate(dests):
        owners = lax.axis_size(axes[layer][0]) * lax.axis_size(axes[layer][1])
        per_block = dest.shape[0] // blocks
        routes.append((owners, -(-dest.shape[0] // owners), patch_blocks * per_block, per_block, block // per_block))
    planes = 4
    if lax.axis_size("gx") == 2:
        index = lax.axis_index("gx")
        flags = jnp.stack([index == 1, index == 0]).astype(jnp.int32)
    else:
        flags = jnp.ones((2,), jnp.int32)
    faces_sent = 1 if lax.axis_size("gx") == 2 else 2
    placed = [(sds((CELLS, channels), BF16), "v"), (sds((faces_sent, VZ * VY, channels), BF16), "v")]
    placed += [(sds((2, PLANE, channels), BF16), "v")]
    placed += [(sds(conv_weight.shape[1:], BF16), "v")]
    weight_sems = pltpu.SemaphoreType.DMA((3,))
    rows_scratch = pltpu.VMEM((slot_count, channels), BF16)
    stream_scratch = pltpu.VMEM((slot_count, channels), F32)
    row_sems = pltpu.SemaphoreType.DMA((row_groups(slot_count),))
    pad_scratch = pltpu.VMEM((PX, VZ + 2, VY, channels), BF16)
    half_conv = CELLS // 2 * 27 * channels * channels * 2

    def route_scratch(layer):
        return [pltpu.SMEM((dests[layer].shape[0],), jnp.int32), pltpu.SMEM((routes[layer][0],), jnp.int32)]

    first = backs = None
    for layer in range(2):
        route = routes[layer]
        owners, capacity, per_owner, per_block, unit = route
        if layer == 0:
            own, xmsg, ymsg, weights = call(
                functools.partial(place_first_kernel, layer, block),
                placed,
                [(flags, "s"), (count, "s"), (vox_block, "v"), (stream, "v"), (conv_weight, "h")],
                [rows_scratch, weight_sems],
                "place0",
                44,
            )
        else:
            own, xmsg, ymsg, weights, stream = call(
                functools.partial(place_next_kernel, layer, routes[layer - 1]),
                placed + [(sds((slot_count, channels), F32), "v")],
                [(flags, "s"), (count, "s"), (dests[layer - 1], "s"), (vox_block, "v"), (first, "h")]
                + [(b, "v") for b in backs]
                + [(conv_weight, "h")],
                [rows_scratch, rows_scratch] + route_scratch(layer - 1) + [row_sems, weight_sems],
                "place1",
                44,
            )
        own = own.reshape(VX, VZ, VY, channels)
        xlo, xhi = exchange_x(xmsg.reshape(-1, VZ, VY, channels))
        middle = call(
            functools.partial(conv_middle_kernel, planes),
            [(sds((CELLS - 2 * planes * VZ * VY, channels), BF16), "v")],
            [(own, "v"), (weights, "v")],
            [pad_scratch],
            "conv_middle",
            24,
            half_conv,
        )
        zshape = (sds((PX, VY, channels), BF16), "v")
        faces = [
            (own, pl.BlockSpec((VX, None, VY, channels), lambda i, z=z: (0, z, 0, 0), pipeline_mode=pl.Buffered(1)))
            for z in (0, VZ - 1)
        ]
        zlow, zhigh = call(
            zface_kernel, [zshape, zshape], [(middle, "h"), (flags, "s")] + faces + [(xlo, "v"), (xhi, "v")], (), "zface", 8
        )
        zlo, zhi = up_down("gz", zlow, zhigh)
        ends = call(
            functools.partial(conv_ends_kernel, planes),
            [(sds((2 * planes * VZ * VY, channels), BF16), "v")],
            [(flags, "s"), (own, "v"), (xlo, "v"), (xhi, "v"), (weights, "v")],
            [pad_scratch],
            "conv_ends",
            24,
            half_conv,
        )
        yshape = (sds((PLANE, channels), BF16), "v")
        ylow, yhigh = call(
            yface_kernel,
            [yshape, yshape],
            [(ends, "h"), (flags, "s"), (ymsg, "v"), (xlo, "v"), (xhi, "v"), (zlo, "v"), (zhi, "v")],
            [pltpu.VMEM((896, channels), BF16)],
            "yface",
            8,
        )
        ylo, yhi = up_down("gy", ylow, yhigh)
        zc = call(
            conv_z_kernel,
            [(sds((2, VX, VY, channels), F32), "v")],
            [(zlo, "v"), (zhi, "v"), (weights, "v")],
            [],
            "conv_z",
            24,
            half_conv // 4,
        )
        gathered = call(
            functools.partial(gather_kernel, planes),
            [(sds((slot_count, channels), F32), "v")],
            [(vox_block, "v"), (middle, "v"), (ends, "v"), (zc, "v")],
            [pltpu.VMEM((CELLS, channels), BF16)],
            "gather",
            24,
            half_conv // 2,
        )
        slots = owners * capacity
        groups = blocks // next(g for g in (3, 2, 1) if blocks % g == 0)
        first, send = call(
            functools.partial(conv_finish_kernel, route),
            [(sds((HELD * slot_count, channels), BF16), "h"), (sds((slots, unit, channels), BF16), "v")],
            [(count, "s"), (dests[layer], "s"), (vox_block, "v"), (gathered, "v")]
            + [(ylo, "v"), (yhi, "v"), (weights, "v"), (stream, "v")],
            [
                pltpu.VMEM((2 * VX * PZ, channels), BF16),
                rows_scratch,
            ]
            + route_scratch(layer)
            + [pltpu.SemaphoreType.DMA((groups,))],
            "conv_finish",
            24,
        )
        received = lax.all_to_all(send, axes[layer], split_axis=0, concat_axis=0, tiled=True)
        answers = owner_work(received, layer, qkv_weight, proj_weight, up_weight, down_weight)
        backs = [lax.all_to_all(a, axes[layer], split_axis=0, concat_axis=0, tiled=True) for a in answers]
    encoded = call(
        functools.partial(restore_kernel, routes[1]),
        [(sds((slot_count, channels), F32), "h")],
        [(count, "s"), (dests[1], "s"), (first, "h")] + [(b, "v") for b in backs],
        [rows_scratch, stream_scratch] + route_scratch(1) + [row_sems, row_sems],
        "restore",
        60,
    )
    return encoded.reshape(1, 1, 1, slot_count, channels)


def solution(mesh):
    in_specs = (
        P("gx", "gy", "gz", None, None),
        P("gx", "gy", "gz", None),
        P("gx", "gy", "gz"),
        P("gx", "gy", "gz", None),
        P("gx", "gy", "gz", None),
        P(),
        P(),
        P(),
        P(),
        P(),
    )
    out_specs = P("gx", "gy", "gz", None, None)
    return jax.shard_map(body, mesh=mesh, in_specs=in_specs, out_specs=out_specs, check_vma=False)
```
